32 devices in a mesh: section: 1, ctx: 32 (over z, y, x, core).
Axes of the slice: x: 2, y: 2, z: 4, core: 2. Of those that a mesh axis runs over, the one named last changes fastest.
Arguments:
- queries: bfloat16 [1, 4096, 2048], P('section', 'ctx'), may hold values from -26 to 26
- key_states: bfloat16 [1, 4096, 1024], P('section', 'ctx'), may hold values from -4 to 4
- value_states: bfloat16 [1, 4096, 1024], P('section', 'ctx'), may hold values from -5 to 5
- upstream: bfloat16 [1, 4096, 2048], P('section', 'ctx'), may hold values from -5 to 5
- segments: int32 [4096], replicated, may hold values from 0 to 7, never falling along the last dimension, each value on 1 to 2048 neighbouring positions
Outputs:
- query_grad: bfloat16 [1, 4096, 2048], P('section', 'ctx')
- key_grad: bfloat16 [1, 4096, 1024], P('section', 'ctx')
- value_grad: bfloat16 [1, 4096, 1024], P('section', 'ctx')
The draws below stay inside these ranges and needn't reach their ends.
All inputs are finite; a program needn't handle non-finite values.
Results may differ from the reference program's by a relative error of at most 0.0095.
Values may be sent and summed in bfloat16 or wider, within the bound.
A program may use at most 64 MiB of HBM per device.

```python
import math
import jax
import jax.numpy as jnp
import numpy as np
from jax import lax

HQ = 8
KVH = 4
DH = 256
WINDOW = 512
TOK_DEV = 128
SECTIONS = 1
TOKENS = 4096
DOCS = 8
DOC_MOST = 2048


def base_keys(key):
    inner_key = jax.random.fold_in(key, 11)
    array_shape = (SECTIONS, TOKENS, KVH * DH)
    base_draw = jax.random.truncated_normal(inner_key, -4.0, 4.0, array_shape, jnp.float32)
    return base_draw


def draw_key_states(key, part):
    base_draw = base_keys(key)
    return base_draw.astype(jnp.bfloat16)


def draw_queries(key, part):
    array_shape = (SECTIONS, TOKENS, HQ * DH)
    inner_key = jax.random.fold_in(key, 23)
    result = jax.random.truncated_normal(inner_key, -4.0, 4.0, array_shape, jnp.float32)
    return result.astype(jnp.bfloat16)


def block_levels(key, shape, shards, low, top_value):
    factor_of = 1.0
    for axis_at, blocks in shards:
        heights = jax.random.uniform(jax.random.fold_in(jax.random.fold_in(key, 6), axis_at), (blocks,), jnp.float32, low / len(shards), top_value / len(shards))
        factor_of = factor_of * jnp.repeat(jnp.exp(heights), shape[axis_at] // blocks).reshape((-1,) + (1,) * (len(shape) - 1 - axis_at))
    return factor_of


def profile(count, total, limit, lean):
    portions = [(1 << 20) // math.isqrt(standing ** lean) + 1 for standing in range(2, count + 1)]
    spare, given = total - limit - (count - 1), [1] * (count - 1)
    while spare > 0:
        free = [i for i in range(count - 1) if given[i] < limit]
        whole, left = sum([portions[i] for i in free]), spare
        for i in free:
            extra = min(limit - given[i], max(1, left * portions[i] // whole), spare)
            given[i] = given[i] + extra
            spare = spare - extra
    return np.array([limit] + given)


def uneven(key, count, total, reach, skew):
    if count == 2:
        one = jax.random.randint(key, (), max(1, total - reach), min(reach, total - 1) + 1)
        return jnp.stack([one, total - one])
    tallies = jnp.asarray(profile(count, total, reach, skew), jnp.int32)
    pairs = (count - 1) // 2
    donor, taker = tallies[1:1 + 2 * pairs:2], tallies[2:2 + 2 * pairs:2]
    room = jnp.minimum(donor - 1, reach - taker)
    passed = jax.random.randint(jax.random.fold_in(key, 1), (pairs,), 0, 1 << 20) % (room + 1)
    tallies = tallies.at[1:1 + 2 * pairs:2].set(donor - passed).at[2:2 + 2 * pairs:2].set(taker + passed)
    return tallies[jax.random.permutation(jax.random.fold_in(key, 2), count)]


def scatter_about(key, extent, scale, reach, split=(), held_as=jnp.bfloat16):
    level = block_levels(key, extent, split, -0.22, 0.18) if split else 1.0
    entries = jax.random.normal(key, extent, jnp.float32) * scale * level
    return jnp.minimum(jnp.maximum(entries, -reach), reach).astype(held_as)


def setup_inputs(seed: int = 0) -> dict:
    arg_keys = jax.random.split(jax.random.key(seed), 6)
    queries = draw_queries(jax.random.fold_in(arg_keys[5], 71), 0)
    key_states = draw_key_states(jax.random.fold_in(arg_keys[5], 71), 0)
    value_states = scatter_about(arg_keys[2], (SECTIONS, TOKENS, KVH * DH), 1.0, 5.0, ((1, 32),))
    upstream = scatter_about(arg_keys[3], (SECTIONS, TOKENS, HQ * DH), 1.0, 5.0, ((1, 32),))
    segments = jnp.searchsorted(jnp.cumsum(uneven(arg_keys[4], DOCS, TOKENS, DOC_MOST, 1)), jnp.arange(TOKENS), side="right").astype(jnp.int32)
    return dict(queries=queries, key_states=key_states, value_states=value_states, upstream=upstream, segments=segments)


masked_score = -1.0e30


def block_backward(query_block, key_block, value_block, grad_block, query_seg, key_seg, query_pos, key_pos):
    query_rows = query_block.shape[0]
    key_count = key_block.shape[0]
    group_size = HQ // KVH
    score_scale = DH ** -0.5
    query_four = query_block.astype(jnp.float32).reshape(query_rows, KVH, group_size, DH)
    grad_four = grad_block.astype(jnp.float32).reshape(query_rows, KVH, group_size, DH)
    key_three = key_block.astype(jnp.float32).reshape(key_count, KVH, DH)
    value_three = value_block.astype(jnp.float32).reshape(key_count, KVH, DH)
    allowed = (key_pos[None, :] <= query_pos[:, None]) & (query_pos[:, None] - key_pos[None, :] < WINDOW) & (query_seg[:, None] == key_seg[None, :])
    scores = jnp.einsum("rkgd,lkd->kgrl", query_four, key_three) * score_scale
    scores = jnp.where(allowed, scores, masked_score)
    row_max = jnp.max(scores, axis=-1, keepdims=True)
    exp_terms = jnp.where(allowed, jnp.exp(scores - row_max), 0.0)
    probability = exp_terms / jnp.sum(exp_terms, axis=-1, keepdims=True)
    weights = lax.optimization_barrier(probability.astype(jnp.bfloat16)).astype(jnp.float32)
    value_grad = jnp.einsum("kgrl,rkgd->lkd", weights, grad_four)
    prob_grad = jnp.einsum("rkgd,lkd->kgrl", grad_four, value_three)
    row_delta = jnp.sum(probability * prob_grad, axis=-1, keepdims=True)
    score_grad = lax.optimization_barrier((probability * (prob_grad - row_delta) * score_scale).astype(jnp.bfloat16)).astype(jnp.float32)
    query_grad = jnp.einsum("kgrl,lkd->rkgd", score_grad, key_three)
    key_grad = jnp.einsum("kgrl,rkgd->lkd", score_grad, query_four)
    return (query_grad.reshape(query_rows, HQ * DH).astype(jnp.bfloat16),
            key_grad.reshape(key_count, KVH * DH),
            value_grad.reshape(key_count, KVH * DH))


def reference(queries, key_states, value_states, upstream, segments):
    reach_blocks = -(-(WINDOW - 1) // TOK_DEV)
    margin = reach_blocks * TOK_DEV
    block_total = TOKENS // TOK_DEV
    out_grad = jnp.roll(upstream, -1, axis=0)
    seg_whole = segments.astype(jnp.int32)
    seg_padded = jnp.concatenate([jnp.full((margin,), -1, jnp.int32), seg_whole])

    def one_section(arrays):
        query_all, key_all, value_all, grad_all = arrays
        key_padded = jnp.concatenate([jnp.zeros((margin, KVH * DH), key_all.dtype), key_all])
        value_padded = jnp.concatenate([jnp.zeros((margin, KVH * DH), value_all.dtype), value_all])

        def advance(carried, block_index):
            key_acc, value_acc = carried
            start = block_index * TOK_DEV
            query_block = lax.dynamic_slice_in_dim(query_all, start, TOK_DEV, 0)
            grad_block = lax.dynamic_slice_in_dim(grad_all, start, TOK_DEV, 0)
            key_block = lax.dynamic_slice_in_dim(key_padded, start, margin + TOK_DEV, 0)
            value_block = lax.dynamic_slice_in_dim(value_padded, start, margin + TOK_DEV, 0)
            query_seg = lax.dynamic_slice_in_dim(seg_whole, start, TOK_DEV, 0)
            key_seg = lax.dynamic_slice_in_dim(seg_padded, start, margin + TOK_DEV, 0)
            query_pos = start + jnp.arange(TOK_DEV, dtype=jnp.int32)
            key_pos = start - margin + jnp.arange(margin + TOK_DEV, dtype=jnp.int32)
            query_grad, key_part, value_part = block_backward(query_block, key_block, value_block, grad_block, query_seg, key_seg, query_pos, key_pos)
            key_acc = lax.dynamic_update_slice_in_dim(key_acc, lax.dynamic_slice_in_dim(key_acc, start, margin + TOK_DEV, 0) + key_part, start, 0)
            value_acc = lax.dynamic_update_slice_in_dim(value_acc, lax.dynamic_slice_in_dim(value_acc, start, margin + TOK_DEV, 0) + value_part, start, 0)
            return (key_acc, value_acc), query_grad

        zero_acc = jnp.zeros((margin + TOKENS, KVH * DH), jnp.float32)
        (key_acc, value_acc), query_grad = lax.scan(advance, (zero_acc, zero_acc), jnp.arange(block_total, dtype=jnp.int32))
        return (query_grad.reshape(TOKENS, HQ * DH),
                key_acc[margin:].astype(jnp.bfloat16),
                value_acc[margin:].astype(jnp.bfloat16))

    query_grad, key_grad, value_grad = lax.map(one_section, (queries, key_states, value_states, out_grad))
    return (query_grad, key_grad, value_grad)
```

```python
import functools
import math

import jax
import jax.numpy as jnp
from jax import lax
from jax.experimental import pallas as pl
from jax.experimental.pallas import tpu as pltpu
from jax.sharding import PartitionSpec as P

HQ = 8
KVH = 4
DH = 256
WINDOW = 512

MESH = pl.DeviceIdType.MESH
masked_score = -1e30


def kernel(
    count, reach, rows,
    q_in, k_in, v_in, g_in, seg_in,
    dq_out, dk_out, dv_out,
    seg_ref, qb, gb, kb, vb, bias, dsb, acc, sbuf, mbuf, rbuf, pbuf, rpart, dqb,
    local_sem, part_send, part_recv, kv_send, kv_recv, pass_send,
    grad_send, grad_recv, mid_recv, gpart_send, gpart_recv, dq_sem,
):
    bf16, f32 = jnp.bfloat16, jnp.float32
    pairs = count // 2
    far = 2 * reach
    span = far + 1
    heads = KVH // 2
    qhalf = HQ // 2 * DH
    group = HQ // KVH
    me = lax.axis_index("ctx")
    c = me // 2
    k = me % 2
    other = 1 - k
    partner = 2 * c + other
    odd = c % 2 == 1
    even = c % 2 == 0
    beside = c + 1 - 2 * (c % 2)
    behind = c >= 2
    ahead = c + 2 < pairs

    def dev(index):
        return {"ctx": index}

    def cols(index, width):
        return pl.ds(pl.multiple_of(index * width, width), width)

    barrier = pltpu.get_barrier_semaphore()
    pl.semaphore_signal(barrier, inc=1, device_id=dev(partner), device_id_type=MESH)
    for j in range(2):
        pl.semaphore_signal(
            barrier, inc=1, device_id=dev(2 * beside + j), device_id_type=MESH
        )
    for there, ok in ((c - 2, behind), (c + 2, ahead)):

        @pl.when(ok)
        def _():
            for j in range(2):
                pl.semaphore_signal(
                    barrier, inc=1, device_id=dev(2 * there + j), device_id_type=MESH
                )

    greeted = 3 + jnp.where(behind, 2, 0) + jnp.where(ahead, 2, 0)

    def kv_copy(which, d, j, g):
        src, dst = ((k_in, kb), (v_in, vb))[which]
        slot = far - 2 * d + k
        return pltpu.make_async_remote_copy(
            src_ref=src.at[0, :, pl.ds((j * heads + g) * DH, DH)],
            dst_ref=dst.at[g, slot],
            send_sem=kv_send.at[which, d - 1, j, g],
            recv_sem=kv_recv.at[which, g, slot],
            device_id=dev(2 * (c + d) + j),
            device_id_type=MESH,
        )

    def kv_arrival(which, slot, g):
        src, dst = ((k_in, kb), (v_in, vb))[which]
        return pltpu.make_async_remote_copy(
            src_ref=src.at[0, :, pl.ds(0, DH)],
            dst_ref=dst.at[g, slot],
            send_sem=kv_send.at[which, 0, 0, g],
            recv_sem=kv_recv.at[which, g, slot],
            device_id=dev(partner),
            device_id_type=MESH,
        )

    def pass_copy(which, j, g):
        ref = (kb, vb)[which]
        return pltpu.make_async_remote_copy(
            src_ref=ref.at[g, j],
            dst_ref=ref.at[g, far - 2 + j],
            send_sem=pass_send.at[which, j, g],
            recv_sem=kv_recv.at[which, g, far - 2 + j],
            device_id=dev(2 * beside + k),
            device_id_type=MESH,
        )

    seg_copy = pltpu.make_async_copy(seg_in, seg_ref, local_sem.at[4, 0])
    seg_copy.start()
    swaps = ((q_in, qb, group * DH, 0), (g_in, gb, group * DH, 0), (k_in, kb, DH, far), (v_in, vb, DH, far))
    own = [
        [
            pltpu.make_async_copy(
                src.at[0, :, cols(k * heads + g, width)], dst.at[g, base + k], local_sem.at[i, g]
            )
            for i, (src, dst, width, base) in enumerate(swaps)
        ]
        for g in range(heads)
    ]
    for copy in own[0] + own[1]:
        copy.start()

    @pl.when(c < 2)
    def _():
        for slot in range(2):
            kb[:, slot] = jnp.zeros((heads, rows, DH), bf16)
            vb[:, slot] = jnp.zeros((heads, rows, DH), bf16)

    @pl.when(c == 0)
    def _():
        for slot in range(2, far):
            kb[:, slot] = jnp.zeros((heads, rows, DH), bf16)
            vb[:, slot] = jnp.zeros((heads, rows, DH), bf16)

    @pl.when(odd)
    def _():
        rbuf[0] = jnp.zeros(rbuf.shape[1:], bf16)

    @pl.when(c + 2 >= pairs)
    def _():
        rbuf[1] = jnp.zeros(rbuf.shape[1:], bf16)

    pl.semaphore_wait(barrier, greeted)

    swap = [
        [
            pltpu.make_async_remote_copy(
                src_ref=src.at[0, :, cols(other * heads + g, width)],
                dst_ref=dst.at[g, base + k],
                send_sem=part_send.at[i, g],
                recv_sem=part_recv.at[i, g],
                device_id=dev(partner),
                device_id_type=MESH,
            )
            for i, (src, dst, width, base) in enumerate(swaps)
        ]
        for g in range(heads)
    ]
    for g in range(heads):
        for which in range(2):
            for j in range(2):
                for d, ok in ((2, ahead), (1, even)):

                    @pl.when(ok)
                    def _():
                        kv_copy(which, d, j, g).start()

        for copy in swap[g]:
            copy.start()

    def seg_row(slot):
        block = jnp.maximum(2 * c - far + slot, 0)
        return seg_ref[pl.ds(block, 1), :].astype(f32)

    seg_copy.wait()
    key_local = lax.broadcasted_iota(jnp.int32, (rows, rows), 0)
    query_local = lax.broadcasted_iota(jnp.int32, (rows, rows), 1)
    for slot in range(far + 2):
        key_seg = jnp.broadcast_to(seg_row(slot), (rows, rows)).T
        exists = 2 * c - far + slot >= 0
        for qi in range(2):
            at = slot - qi
            if 0 <= at < span:
                back = (far - at) * rows + query_local - key_local
                same = key_seg == jnp.broadcast_to(seg_row(far + qi), (rows, rows))
                allowed = (back >= 0) & (back < WINDOW) & same & exists
                bias[qi, pl.ds(at * rows, rows), :] = jnp.where(allowed, 0.0, masked_score)

    pieces = [(which, j) for which in range(2) for j in range(2)]

    def relay(g, part):
        @pl.when(odd & behind)
        def _():
            for which, j in part:
                kv_arrival(which, j, g).wait_recv()
                pass_copy(which, j, g).start()

    def arrive(g):
        @pl.when(even & behind)
        def _():
            for which, j in pieces:
                kv_arrival(which, j, g).wait_recv()

        for copy in own[g] + swap[g]:
            copy.wait()

        @pl.when(c >= 1)
        def _():
            for which, j in pieces:
                kv_arrival(which, far - 2 + j, g).wait_recv()

    factor = DH**-0.5
    exponent = factor * math.log2(math.e)

    def stacked(ref, qi, g):
        return jnp.concatenate(
            [ref[g, qi, :, pl.ds(h * DH, DH)] for h in range(group)], axis=0
        )

    def keys(ref, qi, g):
        return ref[g, pl.ds(qi, span)].reshape(span * rows, DH)

    def nt(a, b):
        return lax.dot_general(a, b, (((1,), (1,)), ((), ())), preferred_element_type=f32)

    def grad_copy(d, j, g, which):
        return pltpu.make_async_remote_copy(
            src_ref=sbuf.at[far - 2 * d + j, g, which],
            dst_ref=rbuf.at[d - 1, k, g, which],
            send_sem=grad_send.at[d - 1, j, g, which],
            recv_sem=grad_recv.at[d - 1, k, g, which],
            device_id=dev(2 * (c - d) + j),
            device_id_type=MESH,
        )

    def mid_copy(j, g, which):
        return pltpu.make_async_remote_copy(
            src_ref=sbuf.at[far - 2 + j, g, which],
            dst_ref=mbuf.at[j, g, which],
            send_sem=grad_send.at[0, j, g, which],
            recv_sem=mid_recv.at[j, g, which],
            device_id=dev(2 * beside + k),
            device_id_type=MESH,
        )

    def grad_arrival(d, j, g, which):
        return pltpu.make_async_remote_copy(
            src_ref=sbuf.at[0, g, which],
            dst_ref=rbuf.at[d - 1, j, g, which],
            send_sem=grad_send.at[d - 1, 0, g, which],
            recv_sem=grad_recv.at[d - 1, j, g, which],
            device_id=dev(partner),
            device_id_type=MESH,
        )

    def part_copy(g):
        return pltpu.make_async_remote_copy(
            src_ref=pbuf.at[g, other],
            dst_ref=rpart.at[g],
            send_sem=gpart_send.at[g],
            recv_sem=gpart_recv.at[g],
            device_id=dev(partner),
            device_id_type=MESH,
        )

    def combine(g):
        @pl.when(odd & behind)
        def _():
            for j in range(2):
                for which in range(2):
                    mid_copy(j, g, which).wait_recv()
                    total = acc[g, which, j] + mbuf[j, g, which].astype(f32)
                    sbuf[j, g, which] = total.astype(bf16)
                    grad_copy(2, j, g, which).start()

    for g in range(heads):
        if g == 0:
            relay(0, pieces)
        arrive(g)
        for qi in range(2):
            if g == 0 and qi == 1:
                relay(1, pieces[:1])
            q_rows, g_rows = stacked(qb, qi, g), stacked(gb, qi, g)
            k_rows, v_rows = keys(kb, qi, g), keys(vb, qi, g)
            mask = bias[qi]
            scores = nt(k_rows, q_rows) + jnp.concatenate([mask] * group, axis=1)
            prob_grad = nt(v_rows, g_rows)
            top = jnp.max(scores, axis=0, keepdims=True)
            terms = jnp.exp2((scores - top) * exponent)
            inverse = 1.0 / jnp.sum(terms, axis=0, keepdims=True)
            delta = jnp.sum(terms * prob_grad, axis=0, keepdims=True) * inverse
            prob = terms * inverse
            grad = (prob * (prob_grad - delta)).astype(bf16)
            dsb[g, qi] = grad
            dk = jnp.dot(grad, q_rows, preferred_element_type=f32) * factor
            dv = jnp.dot(prob.astype(bf16), g_rows, preferred_element_type=f32)
            for which, part in enumerate((dk, dv)):
                for at in range(span):
                    slot = at + qi
                    piece = part[at * rows : (at + 1) * rows]
                    if qi == 0 and slot > 0:
                        acc[g, which, slot] = piece
                        continue
                    if qi == 1 and slot < far + 1:
                        piece = acc[g, which, slot] + piece
                    if slot < 2:
                        acc[g, which, slot] = piece
                    elif slot < far:
                        sbuf[slot, g, which] = piece.astype(bf16)
                    else:
                        acc[g, which, slot] = piece
                        pbuf[g, slot - far, which] = piece.astype(bf16)

        if g == 0:
            relay(1, pieces[1:])

        @pl.when(odd)
        def _():
            for j in range(2):
                for which in range(2):
                    grad_copy(1, j, g, which).start()

        @pl.when(even & behind)
        def _():
            for j in range(2):
                for which in range(2):
                    mid_copy(j, g, which).start()
            for j in range(2):
                sbuf[j, g] = acc[g, :, j].astype(bf16)
                for which in range(2):
                    grad_copy(2, j, g, which).start()

        part_copy(g).start()

    combine(0)
    for qi in range(2):
        for g in range(heads):
            dq = lax.dot_general(
                dsb[g, qi], keys(kb, qi, g), (((0,), (0,)), ((), ())), preferred_element_type=f32
            )
            dq = (dq * factor).astype(bf16)
            for h in range(group):
                dqb[qi, :, pl.ds((group * g + h) * DH, DH)] = dq[h * rows : (h + 1) * rows]
    dq_local = pltpu.make_async_copy(dqb.at[k], dq_out.at[0, :, cols(k, qhalf)], dq_sem.at[0])
    dq_local.start()
    dq_remote = pltpu.make_async_remote_copy(
        src_ref=dqb.at[other],
        dst_ref=dq_out.at[0, :, cols(k, qhalf)],
        send_sem=dq_sem.at[1],
        recv_sem=dq_sem.at[2],
        device_id=dev(partner),
        device_id_type=MESH,
    )
    dq_remote.start()
    combine(1)

    for g in range(heads):
        part_copy(g).wait()
        for d, ok in ((1, even), (2, ahead)):

            @pl.when(ok)
            def _():
                for j in range(2):
                    for which in range(2):
                        grad_arrival(d, j, g, which).wait_recv()

        for which, out in enumerate((dk_out, dv_out)):
            mine = acc[g, which, far + k]
            theirs = rpart[g, which].astype(f32)
            for d in range(reach):
                mine += rbuf[d, k, g, which].astype(f32)
                theirs += rbuf[d, other, g, which].astype(f32)
            out[0, :, cols(k * heads + g, DH)] = mine.astype(bf16)
            out[0, :, cols(other * heads + g, DH)] = theirs.astype(bf16)

    for d, ok in ((2, ahead), (1, even)):

        @pl.when(ok)
        def _():
            for g in range(heads):
                for which in range(2):
                    for j in range(2):
                        kv_copy(which, d, j, g).wait_send()

    @pl.when(odd & behind)
    def _():
        for g in range(heads):
            for which in range(2):
                for j in range(2):
                    pass_copy(which, j, g).wait_send()

    for d, ok in ((2, behind), (1, odd | behind)):

        @pl.when(ok)
        def _():
            for g in range(heads):
                for j in range(2):
                    for which in range(2):
                        grad_copy(d, j, g, which).wait_send()

    dq_local.wait()
    dq_remote.wait()


def local(queries, key_states, value_states, upstream, segments):
    count = lax.axis_size("ctx")
    sections = lax.axis_size("section")
    rows = queries.shape[1]
    out_grad = upstream
    if sections > 1:
        out_grad = lax.ppermute(
            upstream, "section", [(i, (i - 1) % sections) for i in range(sections)]
        )
    reach = -(-(WINDOW - 1) // (2 * rows))
    assert reach == 2 and count % 4 == 0
    far = 2 * reach
    span = far + 1
    heads = KVH // 2
    group = HQ // KVH
    qhalf = HQ // 2 * DH
    bf16, f32 = jnp.bfloat16, jnp.float32
    dma = pltpu.SemaphoreType.DMA
    hbm = pl.BlockSpec(memory_space=pltpu.HBM)
    vmem = pl.BlockSpec(memory_space=pltpu.VMEM)
    shapes = (
        jax.ShapeDtypeStruct(queries.shape, bf16),
        jax.ShapeDtypeStruct(key_states.shape, bf16),
        jax.ShapeDtypeStruct(value_states.shape, bf16),
    )
    operands = (queries, key_states, value_states, out_grad, segments.reshape(-1, rows))
    operands = [pltpu.with_memory_space_constraint(x, pltpu.HBM) for x in operands]
    return pl.pallas_call(
        functools.partial(kernel, count, reach, rows),
        out_shape=shapes,
        in_specs=[hbm] * 5,
        out_specs=(vmem, vmem, vmem),
        scratch_shapes=[
            pltpu.VMEM((segments.shape[0] // rows, rows), jnp.int32),
            pltpu.VMEM((heads, 2, rows, group * DH), bf16),
            pltpu.VMEM((heads, 2, rows, group * DH), bf16),
            pltpu.VMEM((heads, far + 2, rows, DH), bf16),
            pltpu.VMEM((heads, far + 2, rows, DH), bf16),
            pltpu.VMEM((2, span * rows, rows), f32),
            pltpu.VMEM((heads, 2, span * rows, HQ // KVH * rows), bf16),
            pltpu.VMEM((heads, 2, far + 2, rows, DH), f32),
            pltpu.VMEM((far, heads, 2, rows, DH), bf16),
            pltpu.VMEM((2, heads, 2, rows, DH), bf16),
            pltpu.VMEM((reach, 2, heads, 2, rows, DH), bf16),
            pltpu.VMEM((heads, 2, 2, rows, DH), bf16),
            pltpu.VMEM((heads, 2, rows, DH), bf16),
            pltpu.VMEM((2, rows, qhalf), bf16),
            dma((5, heads)),
            dma((4, heads)),
            dma((4, heads)),
            dma((2, reach, 2, heads)),
            dma((2, heads, far)),
            dma((2, 2, heads)),
            dma((reach, 2, heads, 2)),
            dma((reach, 2, heads, 2)),
            dma((2, heads, 2)),
            dma((heads,)),
            dma((heads,)),
            dma((3,)),
        ],
        compiler_params=pltpu.CompilerParams(
            collective_id=0, has_side_effects=True, vmem_limit_bytes=32 * 1024 * 1024
        ),
    )(*operands)


def solution(mesh):
    split = P("section", "ctx", None)
    return jax.shard_map(
        local,
        mesh=mesh,
        in_specs=(split, split, split, split, P()),
        out_specs=(split, split, split),
        check_vma=False,
    )
```

```python
import functools
import math

import jax
import jax.numpy as jnp
from jax import lax
from jax.experimental import pallas as pl
from jax.experimental.pallas import tpu as pltpu
from jax.sharding import PartitionSpec as P

HQ = 8
KVH = 4
DH = 256
WINDOW = 512

MESH = pl.DeviceIdType.MESH
masked_score = -1e30


def kernel(
    count, reach, rows,
    q_in, k_in, v_in, g_in, seg_in,
    dq_out, dk_out, dv_out,
    seg_ref, qb, gb, kb, vb, bias, dsb, acc, sbuf, mbuf, rbuf, pbuf, rpart, dqb,
    local_sem, part_send, part_recv, kv_send, kv_recv, pass_send,
    grad_send, grad_recv, mid_recv, gpart_send, gpart_recv, dq_sem,
):
    bf16, f32 = jnp.bfloat16, jnp.float32
    pairs = count // 2
    far = 2 * reach
    span = far + 1
    heads = KVH // 2
    qhalf = HQ // 2 * DH
    group = HQ // KVH
    me = lax.axis_index("ctx")
    c = me // 2
    k = me % 2
    other = 1 - k
    partner = 2 * c + other
    odd = c % 2 == 1
    even = c % 2 == 0
    beside = c + 1 - 2 * (c % 2)
    behind = c >= 2
    ahead = c + 2 < pairs

    def dev(index):
        return {"ctx": index}

    def cols(index, width):
        return pl.ds(pl.multiple_of(index * width, width), width)

    barrier = pltpu.get_barrier_semaphore()
    pl.semaphore_signal(barrier, inc=1, device_id=dev(partner), device_id_type=MESH)
    for j in range(2):
        pl.semaphore_signal(
            barrier, inc=1, device_id=dev(2 * beside + j), device_id_type=MESH
        )
    for there, ok in ((c - 2, behind), (c + 2, ahead)):

        @pl.when(ok)
        def _():
            for j in range(2):
                pl.semaphore_signal(
                    barrier, inc=1, device_id=dev(2 * there + j), device_id_type=MESH
                )

    greeted = 3 + jnp.where(behind, 2, 0) + jnp.where(ahead, 2, 0)

    def kv_copy(which, d, j, g):
        src, dst = ((k_in, kb), (v_in, vb))[which]
        slot = far - 2 * d + k
        return pltpu.make_async_remote_copy(
            src_ref=src.at[0, :, pl.ds((j * heads + g) * DH, DH)],
            dst_ref=dst.at[g, slot],
            send_sem=kv_send.at[which, d - 1, j, g],
            recv_sem=kv_recv.at[which, g, slot],
            device_id=dev(2 * (c + d) + j),
            device_id_type=MESH,
        )

    def kv_arrival(which, slot, g):
        src, dst = ((k_in, kb), (v_in, vb))[which]
        return pltpu.make_async_remote_copy(
            src_ref=src.at[0, :, pl.ds(0, DH)],
            dst_ref=dst.at[g, slot],
            send_sem=kv_send.at[which, 0, 0, g],
            recv_sem=kv_recv.at[which, g, slot],
            device_id=dev(partner),
            device_id_type=MESH,
        )

    def pass_copy(which, j, g):
        ref = (kb, vb)[which]
        return pltpu.make_async_remote_copy(
            src_ref=ref.at[g, j],
            dst_ref=ref.at[g, far - 2 + j],
            send_sem=pass_send.at[which, j, g],
            recv_sem=kv_recv.at[which, g, far - 2 + j],
            device_id=dev(2 * beside + k),
            device_id_type=MESH,
        )

    seg_copy = pltpu.make_async_copy(seg_in, seg_ref, local_sem.at[4, 0])
    seg_copy.start()
    swaps = ((q_in, qb, group * DH, 0), (g_in, gb, group * DH, 0), (k_in, kb, DH, far), (v_in, vb, DH, far))
    own = [
        [
            pltpu.make_async_copy(
                src.at[0, :, cols(k * heads + g, width)], dst.at[g, base + k], local_sem.at[i, g]
            )
            for i, (src, dst, width, base) in enumerate(swaps)
        ]
        for g in range(heads)
    ]
    for copy in own[0] + own[1]:
        copy.start()

    @pl.when(c < 2)
    def _():
        for slot in range(2):
            kb[:, slot] = jnp.zeros((heads, rows, DH), bf16)
            vb[:, slot] = jnp.zeros((heads, rows, DH), bf16)

    @pl.when(c == 0)
    def _():
        for slot in range(2, far):
            kb[:, slot] = jnp.zeros((heads, rows, DH), bf16)
            vb[:, slot] = jnp.zeros((heads, rows, DH), bf16)

    @pl.when(odd)
    def _():
        rbuf[0] = jnp.zeros(rbuf.shape[1:], bf16)

    @pl.when(c + 2 >= pairs)
    def _():
        rbuf[1] = jnp.zeros(rbuf.shape[1:], bf16)

    pl.semaphore_wait(barrier, greeted)

    swap = [
        [
            pltpu.make_async_remote_copy(
                src_ref=src.at[0, :, cols(other * heads + g, width)],
                dst_ref=dst.at[g, base + k],
                send_sem=part_send.at[i, g],
                recv_sem=part_recv.at[i, g],
                device_id=dev(partner),
                device_id_type=MESH,
            )
            for i, (src, dst, width, base) in enumerate(swaps)
        ]
        for g in range(heads)
    ]
    for g in range(heads):
        for which in range(2):
            for j in range(2):
                for d, ok in ((2, ahead), (1, even)):

                    @pl.when(ok)
                    def _():
                        kv_copy(which, d, j, g).start()

        for copy in swap[g]:
            copy.start()

    def seg_row(slot):
        block = jnp.maximum(2 * c - far + slot, 0)
        return seg_ref[pl.ds(block, 1), :].astype(f32)

    seg_copy.wait()
    key_local = lax.broadcasted_iota(jnp.int32, (rows, rows), 0)
    query_local = lax.broadcasted_iota(jnp.int32, (rows, rows), 1)
    for slot in range(far + 2):
        key_seg = jnp.broadcast_to(seg_row(slot), (rows, rows)).T
        exists = 2 * c - far + slot >= 0
        for qi in range(2):
            at = slot - qi
            if 0 <= at < span:
                back = (far - at) * rows + query_local - key_local
                same = key_seg == jnp.broadcast_to(seg_row(far + qi), (rows, rows))
                allowed = (back >= 0) & (back < WINDOW) & same & exists
                bias[qi, pl.ds(at * rows, rows), :] = jnp.where(allowed, 0.0, masked_score)

    pieces = [(which, j) for which in range(2) for j in range(2)]

    def relay(g, part):
        @pl.when(odd & behind)
        def _():
            for which, j in part:
                kv_arrival(which, j, g).wait_recv()
                pass_copy(which, j, g).start()

    def arrive(g):
        @pl.when(even & behind)
        def _():
            for which, j in pieces:
                kv_arrival(which, j, g).wait_recv()

        for copy in own[g] + swap[g]:
            copy.wait()

        @pl.when(c >= 1)
        def _():
            for which, j in pieces:
                kv_arrival(which, far - 2 + j, g).wait_recv()

    factor = DH**-0.5
    exponent = factor * math.log2(math.e)

    def stacked(ref, qi, g):
        return jnp.concatenate(
            [ref[g, qi, :, pl.ds(h * DH, DH)] for h in range(group)], axis=0
        )

    def keys(ref, qi, g):
        return ref[g, pl.ds(qi, span)].reshape(span * rows, DH)

    def nt(a, b):
        return lax.dot_general(a, b, (((1,), (1,)), ((), ())), preferred_element_type=f32)

    def grad_copy(d, j, g, which):
        return pltpu.make_async_remote_copy(
            src_ref=sbuf.at[far - 2 * d + j, g, which],
            dst_ref=rbuf.at[d - 1, k, g, which],
            send_sem=grad_send.at[d - 1, j, g, which],
            recv_sem=grad_recv.at[d - 1, k, g, which],
            device_id=dev(2 * (c - d) + j),
            device_id_type=MESH,
        )

    def mid_copy(j, g, which):
        return pltpu.make_async_remote_copy(
            src_ref=sbuf.at[far - 2 + j, g, which],
            dst_ref=mbuf.at[j, g, which],
            send_sem=grad_send.at[0, j, g, which],
            recv_sem=mid_recv.at[j, g, which],
            device_id=dev(2 * beside + k),
            device_id_type=MESH,
        )

    def grad_arrival(d, j, g, which):
        return pltpu.make_async_remote_copy(
            src_ref=sbuf.at[0, g, which],
            dst_ref=rbuf.at[d - 1, j, g, which],
            send_sem=grad_send.at[d - 1, 0, g, which],
            recv_sem=grad_recv.at[d - 1, j, g, which],
            device_id=dev(partner),
            device_id_type=MESH,
        )

    def part_copy(g):
        return pltpu.make_async_remote_copy(
            src_ref=pbuf.at[g, other],
            dst_ref=rpart.at[g],
            send_sem=gpart_send.at[g],
            recv_sem=gpart_recv.at[g],
            device_id=dev(partner),
            device_id_type=MESH,
        )

    def combine(g):
        @pl.when(odd & behind)
        def _():
            for j in range(2):
                for which in range(2):
                    mid_copy(j, g, which).wait_recv()
                    total = acc[g, which, j] + mbuf[j, g, which].astype(f32)
                    sbuf[j, g, which] = total.astype(bf16)
                    grad_copy(2, j, g, which).start()

    for g in range(heads):
        if g == 0:
            relay(0, pieces)
        arrive(g)
        for qi in range(2):
            if g == 0 and qi == 1:
                relay(1, pieces[:1])
            q_rows, g_rows = stacked(qb, qi, g), stacked(gb, qi, g)
            k_rows, v_rows = keys(kb, qi, g), keys(vb, qi, g)
            mask = bias[qi]
            scores = nt(k_rows, q_rows) + jnp.concatenate([mask] * group, axis=1)
            prob_grad = nt(v_rows, g_rows)
            top = jnp.max(scores, axis=0, keepdims=True)
            terms = jnp.exp2((scores - top) * exponent)
            inverse = 1.0 / jnp.sum(terms, axis=0, keepdims=True)
            delta = jnp.sum(terms * prob_grad, axis=0, keepdims=True) * inverse
            prob = terms * inverse
            grad = (prob * (prob_grad - delta)).astype(bf16)
            dsb[g, qi] = grad
            dk = jnp.dot(grad, q_rows, preferred_element_type=f32) * factor
            dv = jnp.dot(prob.astype(bf16), g_rows, preferred_element_type=f32)
            for which, part in enumerate((dk, dv)):
                for at in range(span):
                    slot = at + qi
                    piece = part[at * rows : (at + 1) * rows]
                    if qi == 0 and slot > 0:
                        acc[g, which, slot] = piece
                        continue
                    if qi == 1 and slot < far + 1:
                        piece = acc[g, which, slot] + piece
                    if slot < 2:
                        acc[g, which, slot] = piece
                    elif slot < far:
                        sbuf[slot, g, which] = piece.astype(bf16)
                    else:
                        acc[g, which, slot] = piece
                        pbuf[g, slot - far, which] = piece.astype(bf16)

        if g == 0:
            relay(1, pieces[1:])

        @pl.when(odd)
        def _():
            for j in range(2):
                for which in range(2):
                    grad_copy(1, j, g, which).start()

        @pl.when(even & behind)
        def _():
            for j in range(2):
                for which in range(2):
                    mid_copy(j, g, which).start()
            for j in range(2):
                sbuf[j, g] = acc[g, :, j].astype(bf16)
                for which in range(2):
                    grad_copy(2, j, g, which).start()

        part_copy(g).start()

    combine(0)
    for qi in range(2):
        for g in range(heads):
            dq = lax.dot_general(
                dsb[g, qi], keys(kb, qi, g), (((0,), (0,)), ((), ())), preferred_element_type=f32
            )
            dq = (dq * factor).astype(bf16)
            for h in range(group):
                dqb[qi, :, pl.ds((group * g + h) * DH, DH)] = dq[h * rows : (h + 1) * rows]
    dq_local = pltpu.make_async_copy(dqb.at[k], dq_out.at[0, :, cols(k, qhalf)], dq_sem.at[0])
    dq_local.start()
    dq_remote = pltpu.make_async_remote_copy(
        src_ref=dqb.at[other],
        dst_ref=dq_out.at[0, :, cols(k, qhalf)],
        send_sem=dq_sem.at[1],
        recv_sem=dq_sem.at[2],
        device_id=dev(partner),
        device_id_type=MESH,
    )
    dq_remote.start()
    combine(1)

    for g in range(heads):
        part_copy(g).wait()
        for d, ok in ((1, even), (2, ahead)):

            @pl.when(ok)
            def _():
                for j in range(2):
                    for which in range(2):
                        grad_arrival(d, j, g, which).wait_recv()

        for which, out in enumerate((dk_out, dv_out)):
            mine = acc[g, which, far + k]
            theirs = rpart[g, which].astype(f32)
            for d in range(reach):
                mine += rbuf[d, k, g, which].astype(f32)
                theirs += rbuf[d, other, g, which].astype(f32)
            out[0, :, cols(k * heads + g, DH)] = mine.astype(bf16)
            out[0, :, cols(other * heads + g, DH)] = theirs.astype(bf16)

    for d, ok in ((2, ahead), (1, even)):

        @pl.when(ok)
        def _():
            for g in range(heads):
                for which in range(2):
                    for j in range(2):
                        kv_copy(which, d, j, g).wait_send()

    @pl.when(odd & behind)
    def _():
        for g in range(heads):
            for which in range(2):
                for j in range(2):
                    pass_copy(which, j, g).wait_send()

    for d, ok in ((2, behind), (1, odd | behind)):

        @pl.when(ok)
        def _():
            for g in range(heads):
                for j in range(2):
                    for which in range(2):
                        grad_copy(d, j, g, which).wait_send()

    dq_local.wait()
    dq_remote.wait()


def local(queries, key_states, value_states, upstream, segments):
    count = lax.axis_size("ctx")
    sections = lax.axis_size("section")
    rows = queries.shape[1]
    out_grad = upstream
    if sections > 1:
        out_grad = lax.ppermute(
            upstream, "section", [(i, (i - 1) % sections) for i in range(sections)]
        )
    reach = -(-(WINDOW - 1) // (2 * rows))
    assert reach == 2 and count % 4 == 0
    far = 2 * reach
    span = far + 1
    heads = KVH // 2
    group = HQ // KVH
    qhalf = HQ // 2 * DH
    bf16, f32 = jnp.bfloat16, jnp.float32
    dma = pltpu.SemaphoreType.DMA
    hbm = pl.BlockSpec(memory_space=pltpu.HBM)
    vmem = pl.BlockSpec(memory_space=pltpu.VMEM)
    shapes = (
        jax.ShapeDtypeStruct(queries.shape, bf16),
        jax.ShapeDtypeStruct(key_states.shape, bf16),
        jax.ShapeDtypeStruct(value_states.shape, bf16),
    )
    operands = (queries, key_states, value_states, out_grad, segments.reshape(-1, rows))
    operands = [pltpu.with_memory_space_constraint(x, pltpu.HBM) for x in operands]
    results = pl.pallas_call(
        functools.partial(kernel, count, reach, rows),
        out_shape=shapes,
        in_specs=[hbm] * 5,
        out_specs=(vmem, vmem, vmem),
        scratch_shapes=[
            pltpu.VMEM((segments.shape[0] // rows, rows), jnp.int32),
            pltpu.VMEM((heads, 2, rows, group * DH), bf16),
            pltpu.VMEM((heads, 2, rows, group * DH), bf16),
            pltpu.VMEM((heads, far + 2, rows, DH), bf16),
            pltpu.VMEM((heads, far + 2, rows, DH), bf16),
            pltpu.VMEM((2, span * rows, rows), f32),
            pltpu.VMEM((heads, 2, span * rows, HQ // KVH * rows), bf16),
            pltpu.VMEM((heads, 2, far + 2, rows, DH), f32),
            pltpu.VMEM((far, heads, 2, rows, DH), bf16),
            pltpu.VMEM((2, heads, 2, rows, DH), bf16),
            pltpu.VMEM((reach, 2, heads, 2, rows, DH), bf16),
            pltpu.VMEM((heads, 2, 2, rows, DH), bf16),
            pltpu.VMEM((heads, 2, rows, DH), bf16),
            pltpu.VMEM((2, rows, qhalf), bf16),
            dma((5, heads)),
            dma((4, heads)),
            dma((4, heads)),
            dma((2, reach, 2, heads)),
            dma((2, heads, far)),
            dma((2, 2, heads)),
            dma((reach, 2, heads, 2)),
            dma((reach, 2, heads, 2)),
            dma((2, heads, 2)),
            dma((heads,)),
            dma((heads,)),
            dma((3,)),
        ],
        compiler_params=pltpu.CompilerParams(
            collective_id=0, has_side_effects=True, vmem_limit_bytes=32 * 1024 * 1024
        ),
    )(*operands)
    return pl.pallas_call(
        emit,
        out_shape=shapes,
        in_specs=[pl.BlockSpec(memory_space=pl.ANY)] * 3,
        out_specs=[hbm] * 3,
        scratch_shapes=[dma((3,))],
        compiler_params=pltpu.CompilerParams(vmem_limit_bytes=1024 * 1024),
    )(*results)


def emit(a, b, c, a_out, b_out, c_out, sems):
    copies = [
        pltpu.make_async_copy(src, dst, sems.at[i])
        for i, (src, dst) in enumerate(((a, a_out), (b, b_out), (c, c_out)))
    ]
    for copy in copies:
        copy.start()
    for copy in copies:
        copy.wait()


def solution(mesh):
    split = P("section", "ctx", None)
    return jax.shard_map(
        local,
        mesh=mesh,
        in_specs=(split, split, split, split, P()),
        out_specs=(split, split, split),
        check_vma=False,
    )
```

```python
import functools
import math

import jax
import jax.numpy as jnp
from jax import lax
from jax.experimental import pallas as pl
from jax.experimental.pallas import tpu as pltpu
from jax.sharding import PartitionSpec as P

HQ = 8
KVH = 4
DH = 256
WINDOW = 512

MESH = pl.DeviceIdType.MESH
masked_score = -1e30


def kernel(
    count, reach, rows,
    q_in, k_in, v_in, g_in, seg_in,
    dq_out, dk_out, dv_out,
    seg_ref, qb, gb, kb, vb, bias, dsb, acc, sbuf, mbuf, rbuf, pbuf, rpart, dqb,
    local_sem, part_send, part_recv, kv_send, kv_recv, pass_send,
    grad_send, grad_recv, mid_recv, gpart_send, gpart_recv, dq_sem,
):
    bf16, f32 = jnp.bfloat16, jnp.float32
    pairs = count // 2
    far = 2 * reach
    span = far + 1
    heads = KVH // 2
    qhalf = HQ // 2 * DH
    group = HQ // KVH
    me = lax.axis_index("ctx")
    c = me // 2
    k = me % 2
    other = 1 - k
    partner = 2 * c + other
    odd = c % 2 == 1
    even = c % 2 == 0
    beside = c + 1 - 2 * (c % 2)
    behind = c >= 2
    ahead = c + 2 < pairs

    def dev(index):
        return {"ctx": index}

    def cols(index, width):
        return pl.ds(pl.multiple_of(index * width, width), width)

    barrier = pltpu.get_barrier_semaphore()
    pl.semaphore_signal(barrier, inc=1, device_id=dev(partner), device_id_type=MESH)
    for j in range(2):
        pl.semaphore_signal(
            barrier, inc=1, device_id=dev(2 * beside + j), device_id_type=MESH
        )
    for there, ok in ((c - 2, behind), (c + 2, ahead)):

        @pl.when(ok)
        def _():
            for j in range(2):
                pl.semaphore_signal(
                    barrier, inc=1, device_id=dev(2 * there + j), device_id_type=MESH
                )

    greeted = 3 + jnp.where(behind, 2, 0) + jnp.where(ahead, 2, 0)

    def kv_copy(which, d, j, g):
        src, dst = ((k_in, kb), (v_in, vb))[which]
        slot = far - 2 * d + k
        return pltpu.make_async_remote_copy(
            src_ref=src.at[0, :, pl.ds((j * heads + g) * DH, DH)],
            dst_ref=dst.at[g, slot],
            send_sem=kv_send.at[which, d - 1, j, g],
            recv_sem=kv_recv.at[which, g, slot],
            device_id=dev(2 * (c + d) + j),
            device_id_type=MESH,
        )

    def kv_arrival(which, slot, g):
        src, dst = ((k_in, kb), (v_in, vb))[which]
        return pltpu.make_async_remote_copy(
            src_ref=src.at[0, :, pl.ds(0, DH)],
            dst_ref=dst.at[g, slot],
            send_sem=kv_send.at[which, 0, 0, g],
            recv_sem=kv_recv.at[which, g, slot],
            device_id=dev(partner),
            device_id_type=MESH,
        )

    def pass_copy(which, j, g):
        ref = (kb, vb)[which]
        return pltpu.make_async_remote_copy(
            src_ref=ref.at[g, j],
            dst_ref=ref.at[g, far - 2 + j],
            send_sem=pass_send.at[which, j, g],
            recv_sem=kv_recv.at[which, g, far - 2 + j],
            device_id=dev(2 * beside + k),
            device_id_type=MESH,
        )

    seg_copy = pltpu.make_async_copy(seg_in, seg_ref, local_sem.at[4, 0])
    seg_copy.start()
    swaps = ((q_in, qb, group * DH, 0), (g_in, gb, group * DH, 0), (k_in, kb, DH, far), (v_in, vb, DH, far))
    own = [
        [
            pltpu.make_async_copy(
                src.at[0, :, cols(k * heads + g, width)], dst.at[g, base + k], local_sem.at[i, g]
            )
            for i, (src, dst, width, base) in enumerate(swaps)
        ]
        for g in range(heads)
    ]
    for copy in own[0] + own[1]:
        copy.start()

    @pl.when(c < 2)
    def _():
        for slot in range(2):
            kb[:, slot] = jnp.zeros((heads, rows, DH), bf16)
            vb[:, slot] = jnp.zeros((heads, rows, DH), bf16)

    @pl.when(c == 0)
    def _():
        for slot in range(2, far):
            kb[:, slot] = jnp.zeros((heads, rows, DH), bf16)
            vb[:, slot] = jnp.zeros((heads, rows, DH), bf16)

    @pl.when(odd)
    def _():
        rbuf[0] = jnp.zeros(rbuf.shape[1:], bf16)

    @pl.when(c + 2 >= pairs)
    def _():
        rbuf[1] = jnp.zeros(rbuf.shape[1:], bf16)

    pl.semaphore_wait(barrier, greeted)

    swap = [
        [
            pltpu.make_async_remote_copy(
                src_ref=src.at[0, :, cols(other * heads + g, width)],
                dst_ref=dst.at[g, base + k],
                send_sem=part_send.at[i, g],
                recv_sem=part_recv.at[i, g],
                device_id=dev(partner),
                device_id_type=MESH,
            )
            for i, (src, dst, width, base) in enumerate(swaps)
        ]
        for g in range(heads)
    ]
    for g in range(heads):
        for j in range(2):
            for which in range(2):
                for d, ok in ((2, ahead), (1, even)):

                    @pl.when(ok)
                    def _():
                        kv_copy(which, d, j, g).start()

        for copy in swap[g]:
            copy.start()

    def seg_row(slot):
        block = jnp.maximum(2 * c - far + slot, 0)
        return seg_ref[pl.ds(block, 1), :].astype(f32)

    seg_copy.wait()
    key_local = lax.broadcasted_iota(jnp.int32, (rows, rows), 0)
    query_local = lax.broadcasted_iota(jnp.int32, (rows, rows), 1)
    for slot in range(far + 2):
        key_seg = jnp.broadcast_to(seg_row(slot), (rows, rows)).T
        exists = 2 * c - far + slot >= 0
        for qi in range(2):
            at = slot - qi
            if 0 <= at < span:
                back = (far - at) * rows + query_local - key_local
                same = key_seg == jnp.broadcast_to(seg_row(far + qi), (rows, rows))
                allowed = (back >= 0) & (back < WINDOW) & same & exists
                bias[qi, pl.ds(at * rows, rows), :] = jnp.where(allowed, 0.0, masked_score)

    pieces = [(which, j) for which in range(2) for j in range(2)]

    def relay(g, part):
        @pl.when(odd & behind)
        def _():
            for which, j in part:
                kv_arrival(which, j, g).wait_recv()
                pass_copy(which, j, g).start()

    def arrive(g):
        @pl.when(even & behind)
        def _():
            for which, j in pieces:
                kv_arrival(which, j, g).wait_recv()

        for copy in own[g] + swap[g]:
            copy.wait()

        @pl.when(c >= 1)
        def _():
            for which, j in pieces:
                kv_arrival(which, far - 2 + j, g).wait_recv()

    factor = DH**-0.5
    exponent = factor * math.log2(math.e)

    def stacked(ref, qi, g):
        return jnp.concatenate(
            [ref[g, qi, :, pl.ds(h * DH, DH)] for h in range(group)], axis=0
        )

    def keys(ref, qi, g):
        return ref[g, pl.ds(qi, span)].reshape(span * rows, DH)

    def nt(a, b):
        return lax.dot_general(a, b, (((1,), (1,)), ((), ())), preferred_element_type=f32)

    def grad_copy(d, j, g, which):
        return pltpu.make_async_remote_copy(
            src_ref=sbuf.at[far - 2 * d + j, g, which],
            dst_ref=rbuf.at[d - 1, k, g, which],
            send_sem=grad_send.at[d - 1, j, g, which],
            recv_sem=grad_recv.at[d - 1, k, g, which],
            device_id=dev(2 * (c - d) + j),
            device_id_type=MESH,
        )

    def mid_copy(j, g, which):
        return pltpu.make_async_remote_copy(
            src_ref=sbuf.at[far - 2 + j, g, which],
            dst_ref=mbuf.at[j, g, which],
            send_sem=grad_send.at[0, j, g, which],
            recv_sem=mid_recv.at[j, g, which],
            device_id=dev(2 * beside + k),
            device_id_type=MESH,
        )

    def grad_arrival(d, j, g, which):
        return pltpu.make_async_remote_copy(
            src_ref=sbuf.at[0, g, which],
            dst_ref=rbuf.at[d - 1, j, g, which],
            send_sem=grad_send.at[d - 1, 0, g, which],
            recv_sem=grad_recv.at[d - 1, j, g, which],
            device_id=dev(partner),
            device_id_type=MESH,
        )

    def part_copy(g):
        return pltpu.make_async_remote_copy(
            src_ref=pbuf.at[g, other],
            dst_ref=rpart.at[g],
            send_sem=gpart_send.at[g],
            recv_sem=gpart_recv.at[g],
            device_id=dev(partner),
            device_id_type=MESH,
        )

    def combine(g):
        @pl.when(odd & behind)
        def _():
            for j in range(2):
                for which in range(2):
                    mid_copy(j, g, which).wait_recv()
                    total = acc[g, which, j] + mbuf[j, g, which].astype(f32)
                    sbuf[j, g, which] = total.astype(bf16)
                    grad_copy(2, j, g, which).start()

    for g in range(heads):
        if g == 0:
            relay(0, pieces)
        arrive(g)
        for qi in range(2):
            q_rows, g_rows = stacked(qb, qi, g), stacked(gb, qi, g)
            k_rows, v_rows = keys(kb, qi, g), keys(vb, qi, g)
            mask = bias[qi]
            scores = nt(k_rows, q_rows) + jnp.concatenate([mask] * group, axis=1)
            prob_grad = nt(v_rows, g_rows)
            top = jnp.max(scores, axis=0, keepdims=True)
            terms = jnp.exp2((scores - top) * exponent)
            inverse = 1.0 / jnp.sum(terms, axis=0, keepdims=True)
            delta = jnp.sum(terms * prob_grad, axis=0, keepdims=True) * inverse
            prob = terms * inverse
            grad = (prob * (prob_grad - delta)).astype(bf16)
            dsb[g, qi] = grad
            dk = jnp.dot(grad, q_rows, preferred_element_type=f32) * factor
            dv = jnp.dot(prob.astype(bf16), g_rows, preferred_element_type=f32)
            for which, part in enumerate((dk, dv)):
                for at in range(span):
                    slot = at + qi
                    piece = part[at * rows : (at + 1) * rows]
                    if qi == 0 and slot > 0:
                        acc[g, which, slot] = piece
                        continue
                    if qi == 1 and slot < far + 1:
                        piece = acc[g, which, slot] + piece
                    if slot < 2:
                        acc[g, which, slot] = piece
                    elif slot < far:
                        sbuf[slot, g, which] = piece.astype(bf16)
                    else:
                        acc[g, which, slot] = piece
                        pbuf[g, slot - far, which] = piece.astype(bf16)

        if g == 0:
            relay(1, pieces)

        @pl.when(odd)
        def _():
            for j in range(2):
                for which in range(2):
                    grad_copy(1, j, g, which).start()

        @pl.when(even & behind)
        def _():
            for j in range(2):
                for which in range(2):
                    mid_copy(j, g, which).start()
            for j in range(2):
                sbuf[j, g] = acc[g, :, j].astype(bf16)
                for which in range(2):
                    grad_copy(2, j, g, which).start()

        part_copy(g).start()

    combine(0)
    for qi in range(2):
        for g in range(heads):
            dq = lax.dot_general(
                dsb[g, qi], keys(kb, qi, g), (((0,), (0,)), ((), ())), preferred_element_type=f32
            )
            dq = (dq * factor).astype(bf16)
            for h in range(group):
                dqb[qi, :, pl.ds((group * g + h) * DH, DH)] = dq[h * rows : (h + 1) * rows]
    dq_local = pltpu.make_async_copy(dqb.at[k], dq_out.at[0, :, cols(k, qhalf)], dq_sem.at[0])
    dq_local.start()
    dq_remote = pltpu.make_async_remote_copy(
        src_ref=dqb.at[other],
        dst_ref=dq_out.at[0, :, cols(k, qhalf)],
        send_sem=dq_sem.at[1],
        recv_sem=dq_sem.at[2],
        device_id=dev(partner),
        device_id_type=MESH,
    )
    dq_remote.start()
    combine(1)

    for g in range(heads):
        part_copy(g).wait()
        for d, ok in ((1, even), (2, ahead)):

            @pl.when(ok)
            def _():
                for j in range(2):
                    for which in range(2):
                        grad_arrival(d, j, g, which).wait_recv()

        for which, out in enumerate((dk_out, dv_out)):
            mine = acc[g, which, far + k]
            theirs = rpart[g, which].astype(f32)
            for d in range(reach):
                mine += rbuf[d, k, g, which].astype(f32)
                theirs += rbuf[d, other, g, which].astype(f32)
            out[0, :, cols(k * heads + g, DH)] = mine.astype(bf16)
            out[0, :, cols(other * heads + g, DH)] = theirs.astype(bf16)

    for d, ok in ((2, ahead), (1, even)):

        @pl.when(ok)
        def _():
            for g in range(heads):
                for which in range(2):
                    for j in range(2):
                        kv_copy(which, d, j, g).wait_send()

    @pl.when(odd & behind)
    def _():
        for g in range(heads):
            for which in range(2):
                for j in range(2):
                    pass_copy(which, j, g).wait_send()

    for d, ok in ((2, behind), (1, odd | behind)):

        @pl.when(ok)
        def _():
            for g in range(heads):
                for j in range(2):
                    for which in range(2):
                        grad_copy(d, j, g, which).wait_send()

    dq_local.wait()
    dq_remote.wait()


def local(queries, key_states, value_states, upstream, segments):
    count = lax.axis_size("ctx")
    sections = lax.axis_size("section")
    rows = queries.shape[1]
    out_grad = upstream
    if sections > 1:
        out_grad = lax.ppermute(
            upstream, "section", [(i, (i - 1) % sections) for i in range(sections)]
        )
    reach = -(-(WINDOW - 1) // (2 * rows))
    assert reach == 2 and count % 4 == 0
    far = 2 * reach
    span = far + 1
    heads = KVH // 2
    group = HQ // KVH
    qhalf = HQ // 2 * DH
    bf16, f32 = jnp.bfloat16, jnp.float32
    dma = pltpu.SemaphoreType.DMA
    hbm = pl.BlockSpec(memory_space=pltpu.HBM)
    vmem = pl.BlockSpec(memory_space=pltpu.VMEM)
    shapes = (
        jax.ShapeDtypeStruct(queries.shape, bf16),
        jax.ShapeDtypeStruct(key_states.shape, bf16),
        jax.ShapeDtypeStruct(value_states.shape, bf16),
    )
    operands = (queries, key_states, value_states, out_grad, segments.reshape(-1, rows))
    operands = [pltpu.with_memory_space_constraint(x, pltpu.HBM) for x in operands]
    results = pl.pallas_call(
        functools.partial(kernel, count, reach, rows),
        out_shape=shapes,
        in_specs=[hbm] * 5,
        out_specs=(vmem, vmem, vmem),
        scratch_shapes=[
            pltpu.VMEM((segments.shape[0] // rows, rows), jnp.int32),
            pltpu.VMEM((heads, 2, rows, group * DH), bf16),
            pltpu.VMEM((heads, 2, rows, group * DH), bf16),
            pltpu.VMEM((heads, far + 2, rows, DH), bf16),
            pltpu.VMEM((heads, far + 2, rows, DH), bf16),
            pltpu.VMEM((2, span * rows, rows), f32),
            pltpu.VMEM((heads, 2, span * rows, HQ // KVH * rows), bf16),
            pltpu.VMEM((heads, 2, far + 2, rows, DH), f32),
            pltpu.VMEM((far, heads, 2, rows, DH), bf16),
            pltpu.VMEM((2, heads, 2, rows, DH), bf16),
            pltpu.VMEM((reach, 2, heads, 2, rows, DH), bf16),
            pltpu.VMEM((heads, 2, 2, rows, DH), bf16),
            pltpu.VMEM((heads, 2, rows, DH), bf16),
            pltpu.VMEM((2, rows, qhalf), bf16),
            dma((5, heads)),
            dma((4, heads)),
            dma((4, heads)),
            dma((2, reach, 2, heads)),
            dma((2, heads, far)),
            dma((2, 2, heads)),
            dma((reach, 2, heads, 2)),
            dma((reach, 2, heads, 2)),
            dma((2, heads, 2)),
            dma((heads,)),
            dma((heads,)),
            dma((3,)),
        ],
        compiler_params=pltpu.CompilerParams(
            collective_id=0, has_side_effects=True, vmem_limit_bytes=32 * 1024 * 1024
        ),
    )(*operands)
    return pl.pallas_call(
        emit,
        out_shape=shapes,
        in_specs=[pl.BlockSpec(memory_space=pl.ANY)] * 3,
        out_specs=[hbm] * 3,
        scratch_shapes=[dma((3,))],
        compiler_params=pltpu.CompilerParams(vmem_limit_bytes=1024 * 1024),
    )(*results)


def emit(a, b, c, a_out, b_out, c_out, sems):
    copies = [
        pltpu.make_async_copy(src, dst, sems.at[i])
        for i, (src, dst) in enumerate(((a, a_out), (b, b_out), (c, c_out)))
    ]
    for copy in copies:
        copy.start()
    for copy in copies:
        copy.wait()


def solution(mesh):
    split = P("section", "ctx", None)
    return jax.shard_map(
        local,
        mesh=mesh,
        in_specs=(split, split, split, split, P()),
        out_specs=(split, split, split),
        check_vma=False,
    )
```

```python
import functools
import math

import jax
import jax.numpy as jnp
from jax import lax
from jax.experimental import pallas as pl
from jax.experimental.pallas import tpu as pltpu
from jax.sharding import PartitionSpec as P

HQ = 8
KVH = 4
DH = 256
WINDOW = 512

MESH = pl.DeviceIdType.MESH
masked_score = -1e30


def kernel(
    count, reach, rows,
    q_in, k_in, v_in, g_in, seg_in,
    dq_out, dk_out, dv_out,
    seg_ref, qb, gb, kb, vb, bias, dsb, acc, probs, sbuf, mbuf, rbuf, pbuf, rpart, dqb,
    local_sem, part_send, part_recv, kv_send, kv_recv, pass_send,
    grad_send, grad_recv, mid_recv, gpart_send, gpart_recv, dq_sem,
):
    bf16, f32 = jnp.bfloat16, jnp.float32
    pairs = count // 2
    far = 2 * reach
    span = far + 1
    heads = KVH // 2
    qhalf = HQ // 2 * DH
    group = HQ // KVH
    me = lax.axis_index("ctx")
    c = me // 2
    k = me % 2
    other = 1 - k
    partner = 2 * c + other
    odd = c % 2 == 1
    even = c % 2 == 0
    beside = c + 1 - 2 * (c % 2)
    behind = c >= 2
    ahead = c + 2 < pairs

    def dev(index):
        return {"ctx": index}

    def cols(index, width):
        return pl.ds(pl.multiple_of(index * width, width), width)

    barrier = pltpu.get_barrier_semaphore()
    pl.semaphore_signal(barrier, inc=1, device_id=dev(partner), device_id_type=MESH)
    for j in range(2):
        pl.semaphore_signal(
            barrier, inc=1, device_id=dev(2 * beside + j), device_id_type=MESH
        )
    for there, ok in ((c - 2, behind), (c + 2, ahead)):

        @pl.when(ok)
        def _():
            for j in range(2):
                pl.semaphore_signal(
                    barrier, inc=1, device_id=dev(2 * there + j), device_id_type=MESH
                )

    greeted = 3 + jnp.where(behind, 2, 0) + jnp.where(ahead, 2, 0)

    def kv_copy(which, d, j, g):
        src, dst = ((k_in, kb), (v_in, vb))[which]
        slot = far - 2 * d + k
        return pltpu.make_async_remote_copy(
            src_ref=src.at[0, :, pl.ds((j * heads + g) * DH, DH)],
            dst_ref=dst.at[g, slot],
            send_sem=kv_send.at[which, d - 1, j, g],
            recv_sem=kv_recv.at[which, g, slot],
            device_id=dev(2 * (c + d) + j),
            device_id_type=MESH,
        )

    def kv_arrival(which, slot, g):
        src, dst = ((k_in, kb), (v_in, vb))[which]
        return pltpu.make_async_remote_copy(
            src_ref=src.at[0, :, pl.ds(0, DH)],
            dst_ref=dst.at[g, slot],
            send_sem=kv_send.at[which, 0, 0, g],
            recv_sem=kv_recv.at[which, g, slot],
            device_id=dev(partner),
            device_id_type=MESH,
        )

    def pass_copy(which, j, g):
        ref = (kb, vb)[which]
        return pltpu.make_async_remote_copy(
            src_ref=ref.at[g, j],
            dst_ref=ref.at[g, far - 2 + j],
            send_sem=pass_send.at[which, j, g],
            recv_sem=kv_recv.at[which, g, far - 2 + j],
            device_id=dev(2 * beside + k),
            device_id_type=MESH,
        )

    seg_copy = pltpu.make_async_copy(seg_in, seg_ref, local_sem.at[4, 0])
    seg_copy.start()
    swaps = ((q_in, qb, group * DH, 0), (g_in, gb, group * DH, 0), (k_in, kb, DH, far), (v_in, vb, DH, far))
    own = [
        [
            pltpu.make_async_copy(
                src.at[0, :, cols(k * heads + g, width)], dst.at[g, base + k], local_sem.at[i, g]
            )
            for i, (src, dst, width, base) in enumerate(swaps)
        ]
        for g in range(heads)
    ]
    for copy in own[0] + own[1]:
        copy.start()

    @pl.when(c < 2)
    def _():
        for slot in range(2):
            kb[:, slot] = jnp.zeros((heads, rows, DH), bf16)
            vb[:, slot] = jnp.zeros((heads, rows, DH), bf16)

    @pl.when(c == 0)
    def _():
        for slot in range(2, far):
            kb[:, slot] = jnp.zeros((heads, rows, DH), bf16)
            vb[:, slot] = jnp.zeros((heads, rows, DH), bf16)

    @pl.when(odd)
    def _():
        rbuf[0] = jnp.zeros(rbuf.shape[1:], bf16)

    @pl.when(c + 2 >= pairs)
    def _():
        rbuf[1] = jnp.zeros(rbuf.shape[1:], bf16)

    pl.semaphore_wait(barrier, greeted)

    swap = [
        [
            pltpu.make_async_remote_copy(
                src_ref=src.at[0, :, cols(other * heads + g, width)],
                dst_ref=dst.at[g, base + k],
                send_sem=part_send.at[i, g],
                recv_sem=part_recv.at[i, g],
                device_id=dev(partner),
                device_id_type=MESH,
            )
            for i, (src, dst, width, base) in enumerate(swaps)
        ]
        for g in range(heads)
    ]
    for g in range(heads):
        for j in range(2):
            for which in range(2):
                for d, ok in ((2, ahead), (1, even)):

                    @pl.when(ok)
                    def _():
                        kv_copy(which, d, j, g).start()

        for copy in swap[g]:
            copy.start()

    def seg_row(slot):
        block = jnp.maximum(2 * c - far + slot, 0)
        return seg_ref[pl.ds(block, 1), :].astype(f32)

    seg_copy.wait()
    key_local = lax.broadcasted_iota(jnp.int32, (rows, rows), 0)
    query_local = lax.broadcasted_iota(jnp.int32, (rows, rows), 1)
    for slot in range(far + 2):
        key_seg = jnp.broadcast_to(seg_row(slot), (rows, rows)).T
        exists = 2 * c - far + slot >= 0
        for qi in range(2):
            at = slot - qi
            if 0 <= at < span:
                back = (far - at) * rows + query_local - key_local
                same = key_seg == jnp.broadcast_to(seg_row(far + qi), (rows, rows))
                allowed = (back >= 0) & (back < WINDOW) & same & exists
                bias[qi, pl.ds(at * rows, rows), :] = jnp.where(allowed, 0.0, masked_score)

    pieces = [(which, j) for which in range(2) for j in range(2)]

    def relay(g, part):
        @pl.when(odd & behind)
        def _():
            for which, j in part:
                kv_arrival(which, j, g).wait_recv()
                pass_copy(which, j, g).start()

    def arrive(g, which):
        @pl.when(even & behind)
        def _():
            for j in range(2):
                kv_arrival(which, j, g).wait_recv()

        for copies in (own[g], swap[g]):
            for copy in copies[3:] if which else copies[:3]:
                copy.wait()

        @pl.when(c >= 1)
        def _():
            for j in range(2):
                kv_arrival(which, far - 2 + j, g).wait_recv()

    factor = DH**-0.5
    exponent = factor * math.log2(math.e)

    def stacked(ref, qi, g):
        return jnp.concatenate(
            [ref[g, qi, :, pl.ds(h * DH, DH)] for h in range(group)], axis=0
        )

    def keys(ref, qi, g):
        return ref[g, pl.ds(qi, span)].reshape(span * rows, DH)

    def nt(a, b):
        return lax.dot_general(a, b, (((1,), (1,)), ((), ())), preferred_element_type=f32)

    def grad_copy(d, j, g, which):
        return pltpu.make_async_remote_copy(
            src_ref=sbuf.at[far - 2 * d + j, g, which],
            dst_ref=rbuf.at[d - 1, k, g, which],
            send_sem=grad_send.at[d - 1, j, g, which],
            recv_sem=grad_recv.at[d - 1, k, g, which],
            device_id=dev(2 * (c - d) + j),
            device_id_type=MESH,
        )

    def mid_copy(j, g, which):
        return pltpu.make_async_remote_copy(
            src_ref=sbuf.at[far - 2 + j, g, which],
            dst_ref=mbuf.at[j, g, which],
            send_sem=grad_send.at[0, j, g, which],
            recv_sem=mid_recv.at[j, g, which],
            device_id=dev(2 * beside + k),
            device_id_type=MESH,
        )

    def grad_arrival(d, j, g, which):
        return pltpu.make_async_remote_copy(
            src_ref=sbuf.at[0, g, which],
            dst_ref=rbuf.at[d - 1, j, g, which],
            send_sem=grad_send.at[d - 1, 0, g, which],
            recv_sem=grad_recv.at[d - 1, j, g, which],
            device_id=dev(partner),
            device_id_type=MESH,
        )

    def part_copy(g):
        return pltpu.make_async_remote_copy(
            src_ref=pbuf.at[g, other],
            dst_ref=rpart.at[g],
            send_sem=gpart_send.at[g],
            recv_sem=gpart_recv.at[g],
            device_id=dev(partner),
            device_id_type=MESH,
        )

    def combine(g):
        @pl.when(odd & behind)
        def _():
            for which in (1, 0):
                for j in range(2):
                    mid_copy(j, g, which).wait_recv()
                    total = acc[g, which, j] + mbuf[j, g, which].astype(f32)
                    sbuf[j, g, which] = total.astype(bf16)
                    grad_copy(2, j, g, which).start()

    def place(g, qi, which, part):
        for at in range(span):
            slot = at + qi
            piece = part[at * rows : (at + 1) * rows]
            if qi == 0 and slot > 0:
                acc[g, which, slot] = piece
                continue
            if qi == 1 and slot < far + 1:
                piece = acc[g, which, slot] + piece
            if slot < 2:
                acc[g, which, slot] = piece
            elif slot < far:
                sbuf[slot, g, which] = piece.astype(bf16)
            else:
                acc[g, which, slot] = piece
                pbuf[g, slot - far, which] = piece.astype(bf16)

    def send_even(g, which):
        @pl.when(even & behind)
        def _():
            for j in range(2):
                mid_copy(j, g, which).start()
            for j in range(2):
                sbuf[j, g, which] = acc[g, which, j].astype(bf16)
                grad_copy(2, j, g, which).start()

    for g in range(heads):
        if g == 0:
            relay(0, pieces)
        arrive(g, 0)
        for qi in range(2):
            q_rows, g_rows = stacked(qb, qi, g), stacked(gb, qi, g)
            mask = bias[qi]
            scores = nt(keys(kb, qi, g), q_rows) + jnp.concatenate([mask] * group, axis=1)
            top = jnp.max(scores, axis=0, keepdims=True)
            terms = jnp.exp2((scores - top) * exponent)
            inverse = 1.0 / jnp.sum(terms, axis=0, keepdims=True)
            prob = terms * inverse
            probs[qi] = prob
            dv = jnp.dot(prob.astype(bf16), g_rows, preferred_element_type=f32)
            place(g, qi, 1, dv)
        send_even(g, 1)
        arrive(g, 1)
        for qi in range(2):
            q_rows, g_rows = stacked(qb, qi, g), stacked(gb, qi, g)
            prob = probs[qi]
            prob_grad = nt(keys(vb, qi, g), g_rows)
            delta = jnp.sum(prob * prob_grad, axis=0, keepdims=True)
            grad = (prob * (prob_grad - delta)).astype(bf16)
            dsb[g, qi] = grad
            dk = jnp.dot(grad, q_rows, preferred_element_type=f32) * factor
            place(g, qi, 0, dk)
        send_even(g, 0)

        if g == 0:
            relay(1, pieces)

        @pl.when(odd)
        def _():
            for which in (1, 0):
                for j in range(2):
                    grad_copy(1, j, g, which).start()

        part_copy(g).start()

    combine(0)
    for qi in range(2):
        for g in range(heads):
            dq = lax.dot_general(
                dsb[g, qi], keys(kb, qi, g), (((0,), (0,)), ((), ())), preferred_element_type=f32
            )
            dq = (dq * factor).astype(bf16)
            for h in range(group):
                dqb[qi, :, pl.ds((group * g + h) * DH, DH)] = dq[h * rows : (h + 1) * rows]
    dq_local = pltpu.make_async_copy(dqb.at[k], dq_out.at[0, :, cols(k, qhalf)], dq_sem.at[0])
    dq_local.start()
    dq_remote = pltpu.make_async_remote_copy(
        src_ref=dqb.at[other],
        dst_ref=dq_out.at[0, :, cols(k, qhalf)],
        send_sem=dq_sem.at[1],
        recv_sem=dq_sem.at[2],
        device_id=dev(partner),
        device_id_type=MESH,
    )
    dq_remote.start()
    combine(1)

    for g in range(heads):
        part_copy(g).wait()
        for d, ok in ((1, even), (2, ahead)):

            @pl.when(ok)
            def _():
                for j in range(2):
                    for which in range(2):
                        grad_arrival(d, j, g, which).wait_recv()

        for which, out in enumerate((dk_out, dv_out)):
            mine = acc[g, which, far + k]
            theirs = rpart[g, which].astype(f32)
            for d in range(reach):
                mine += rbuf[d, k, g, which].astype(f32)
                theirs += rbuf[d, other, g, which].astype(f32)
            out[0, :, cols(k * heads + g, DH)] = mine.astype(bf16)
            out[0, :, cols(other * heads + g, DH)] = theirs.astype(bf16)

    for d, ok in ((2, ahead), (1, even)):

        @pl.when(ok)
        def _():
            for g in range(heads):
                for which in range(2):
                    for j in range(2):
                        kv_copy(which, d, j, g).wait_send()

    @pl.when(odd & behind)
    def _():
        for g in range(heads):
            for which in range(2):
                for j in range(2):
                    pass_copy(which, j, g).wait_send()

    for d, ok in ((2, behind), (1, odd | behind)):

        @pl.when(ok)
        def _():
            for g in range(heads):
                for j in range(2):
                    for which in range(2):
                        grad_copy(d, j, g, which).wait_send()

    dq_local.wait()
    dq_remote.wait()


def local(queries, key_states, value_states, upstream, segments):
    count = lax.axis_size("ctx")
    sections = lax.axis_size("section")
    rows = queries.shape[1]
    out_grad = upstream
    if sections > 1:
        out_grad = lax.ppermute(
            upstream, "section", [(i, (i - 1) % sections) for i in range(sections)]
        )
    reach = -(-(WINDOW - 1) // (2 * rows))
    assert reach == 2 and count % 4 == 0
    far = 2 * reach
    span = far + 1
    heads = KVH // 2
    group = HQ // KVH
    qhalf = HQ // 2 * DH
    bf16, f32 = jnp.bfloat16, jnp.float32
    dma = pltpu.SemaphoreType.DMA
    hbm = pl.BlockSpec(memory_space=pltpu.HBM)
    vmem = pl.BlockSpec(memory_space=pltpu.VMEM)
    shapes = (
        jax.ShapeDtypeStruct(queries.shape, bf16),
        jax.ShapeDtypeStruct(key_states.shape, bf16),
        jax.ShapeDtypeStruct(value_states.shape, bf16),
    )
    operands = (queries, key_states, value_states, out_grad, segments.reshape(-1, rows))
    operands = [pltpu.with_memory_space_constraint(x, pltpu.HBM) for x in operands]
    results = pl.pallas_call(
        functools.partial(kernel, count, reach, rows),
        out_shape=shapes,
        in_specs=[hbm] * 5,
        out_specs=(vmem, vmem, vmem),
        scratch_shapes=[
            pltpu.VMEM((segments.shape[0] // rows, rows), jnp.int32),
            pltpu.VMEM((heads, 2, rows, group * DH), bf16),
            pltpu.VMEM((heads, 2, rows, group * DH), bf16),
            pltpu.VMEM((heads, far + 2, rows, DH), bf16),
            pltpu.VMEM((heads, far + 2, rows, DH), bf16),
            pltpu.VMEM((2, span * rows, rows), f32),
            pltpu.VMEM((heads, 2, span * rows, HQ // KVH * rows), bf16),
            pltpu.VMEM((heads, 2, far + 2, rows, DH), f32),
            pltpu.VMEM((2, span * rows, group * rows), f32),
            pltpu.VMEM((far, heads, 2, rows, DH), bf16),
            pltpu.VMEM((2, heads, 2, rows, DH), bf16),
            pltpu.VMEM((reach, 2, heads, 2, rows, DH), bf16),
            pltpu.VMEM((heads, 2, 2, rows, DH), bf16),
            pltpu.VMEM((heads, 2, rows, DH), bf16),
            pltpu.VMEM((2, rows, qhalf), bf16),
            dma((5, heads)),
            dma((4, heads)),
            dma((4, heads)),
            dma((2, reach, 2, heads)),
            dma((2, heads, far)),
            dma((2, 2, heads)),
            dma((reach, 2, heads, 2)),
            dma((reach, 2, heads, 2)),
            dma((2, heads, 2)),
            dma((heads,)),
            dma((heads,)),
            dma((3,)),
        ],
        compiler_params=pltpu.CompilerParams(
            collective_id=0, has_side_effects=True, vmem_limit_bytes=32 * 1024 * 1024
        ),
    )(*operands)
    return pl.pallas_call(
        emit,
        out_shape=shapes,
        in_specs=[pl.BlockSpec(memory_space=pl.ANY)] * 3,
        out_specs=[hbm] * 3,
        scratch_shapes=[dma((3,))],
        compiler_params=pltpu.CompilerParams(vmem_limit_bytes=1024 * 1024),
    )(*results)


def emit(a, b, c, a_out, b_out, c_out, sems):
    copies = [
        pltpu.make_async_copy(src, dst, sems.at[i])
        for i, (src, dst) in enumerate(((a, a_out), (b, b_out), (c, c_out)))
    ]
    for copy in copies:
        copy.start()
    for copy in copies:
        copy.wait()


def solution(mesh):
    split = P("section", "ctx", None)
    return jax.shard_map(
        local,
        mesh=mesh,
        in_specs=(split, split, split, split, P()),
        out_specs=(split, split, split),
        check_vma=False,
    )
```

```python
import functools
import math

import jax
import jax.numpy as jnp
from jax import lax
from jax.experimental import pallas as pl
from jax.experimental.pallas import tpu as pltpu
from jax.sharding import PartitionSpec as P

HQ = 8
KVH = 4
DH = 256
WINDOW = 512

MESH = pl.DeviceIdType.MESH
masked_score = -1e30


def kernel(
    count, reach, rows,
    q_in, k_in, v_in, g_in, seg_in,
    dq_out, dk_out, dv_out,
    seg_ref, qb, gb, kb, vb, bias, dsb, acc, probs, sbuf, mbuf, rbuf, pbuf, rpart, dqb,
    local_sem, part_send, part_recv, kv_send, kv_recv, pass_send,
    grad_send, grad_recv, mid_recv, gpart_send, gpart_recv, dq_sem,
):
    bf16, f32 = jnp.bfloat16, jnp.float32
    pairs = count // 2
    far = 2 * reach
    span = far + 1
    heads = KVH // 2
    qhalf = HQ // 2 * DH
    group = HQ // KVH
    me = lax.axis_index("ctx")
    c = me // 2
    k = me % 2
    other = 1 - k
    partner = 2 * c + other
    odd = c % 2 == 1
    even = c % 2 == 0
    beside = c + 1 - 2 * (c % 2)
    behind = c >= 2
    ahead = c + 2 < pairs
    hop = odd & (c + 1 < pairs)
    direct = [(0, 0, [(1, 1, 0), (1, 1, 1)], hop & (c % 4 == 1)), (1, 0, [(1, 1, 1)], hop & (c % 4 == 3))]

    def dev(index):
        return {"ctx": index}

    def cols(index, width):
        return pl.ds(pl.multiple_of(index * width, width), width)

    barrier = pltpu.get_barrier_semaphore()
    pl.semaphore_signal(barrier, inc=1, device_id=dev(partner), device_id_type=MESH)
    for j in range(2):
        pl.semaphore_signal(
            barrier, inc=1, device_id=dev(2 * beside + j), device_id_type=MESH
        )
    for there, ok in ((c - 2, behind), (c + 2, ahead)):

        @pl.when(ok)
        def _():
            for j in range(2):
                pl.semaphore_signal(
                    barrier, inc=1, device_id=dev(2 * there + j), device_id_type=MESH
                )

    @pl.when(even & (c >= 1) & (k == 1))
    def _():
        for j in range(2):
            pl.semaphore_signal(
                barrier, inc=1, device_id=dev(2 * (c - 1) + j), device_id_type=MESH
            )

    greeted = 3 + jnp.where(behind, 2, 0) + jnp.where(ahead, 2, 0) + jnp.where(hop, 1, 0)

    def kv_copy(which, d, j, g):
        src, dst = ((k_in, kb), (v_in, vb))[which]
        slot = far - 2 * d + k
        return pltpu.make_async_remote_copy(
            src_ref=src.at[0, :, pl.ds((j * heads + g) * DH, DH)],
            dst_ref=dst.at[g, slot],
            send_sem=kv_send.at[which, d - 1, j, g],
            recv_sem=kv_recv.at[which, g, slot],
            device_id=dev(2 * (c + d) + j),
            device_id_type=MESH,
        )

    def kv_arrival(which, slot, g):
        src, dst = ((k_in, kb), (v_in, vb))[which]
        return pltpu.make_async_remote_copy(
            src_ref=src.at[0, :, pl.ds(0, DH)],
            dst_ref=dst.at[g, slot],
            send_sem=kv_send.at[which, 0, 0, g],
            recv_sem=kv_recv.at[which, g, slot],
            device_id=dev(partner),
            device_id_type=MESH,
        )

    def pass_copy(which, j, g):
        ref = (kb, vb)[which]
        return pltpu.make_async_remote_copy(
            src_ref=ref.at[g, j],
            dst_ref=ref.at[g, far - 2 + j],
            send_sem=pass_send.at[which, j, g],
            recv_sem=kv_recv.at[which, g, far - 2 + j],
            device_id=dev(2 * beside + k),
            device_id_type=MESH,
        )

    seg_copy = pltpu.make_async_copy(seg_in, seg_ref, local_sem.at[4, 0])
    seg_copy.start()
    swaps = ((q_in, qb, group * DH, 0), (g_in, gb, group * DH, 0), (k_in, kb, DH, far), (v_in, vb, DH, far))
    own = [
        [
            pltpu.make_async_copy(
                src.at[0, :, cols(k * heads + g, width)], dst.at[g, base + k], local_sem.at[i, g]
            )
            for i, (src, dst, width, base) in enumerate(swaps)
        ]
        for g in range(heads)
    ]
    for copy in own[0] + own[1]:
        copy.start()

    @pl.when(c < 2)
    def _():
        for slot in range(2):
            kb[:, slot] = jnp.zeros((heads, rows, DH), bf16)
            vb[:, slot] = jnp.zeros((heads, rows, DH), bf16)

    @pl.when(c == 0)
    def _():
        for slot in range(2, far):
            kb[:, slot] = jnp.zeros((heads, rows, DH), bf16)
            vb[:, slot] = jnp.zeros((heads, rows, DH), bf16)

    @pl.when(odd)
    def _():
        rbuf[0] = jnp.zeros(rbuf.shape[1:], bf16)

    @pl.when(c + 2 >= pairs)
    def _():
        rbuf[1] = jnp.zeros(rbuf.shape[1:], bf16)

    pl.semaphore_wait(barrier, greeted)

    swap = [
        [
            pltpu.make_async_remote_copy(
                src_ref=src.at[0, :, cols(other * heads + g, width)],
                dst_ref=dst.at[g, base + k],
                send_sem=part_send.at[i, g],
                recv_sem=part_recv.at[i, g],
                device_id=dev(partner),
                device_id_type=MESH,
            )
            for i, (src, dst, width, base) in enumerate(swaps)
        ]
        for g in range(heads)
    ]
    for g in range(heads):
        for j in range(2):
            for which in range(2):
                for d, ok in ((2, ahead), (1, even)):

                    @pl.when(ok)
                    def _():
                        kv_copy(which, d, j, g).start()

            for *after, copies, ok in direct:
                if after == [g, j]:

                    @pl.when(ok)
                    def _():
                        for head, core, which in copies:
                            kv_copy(which, 1, core, head).start()

        for copy in swap[g]:
            copy.start()

    def seg_row(slot):
        block = jnp.maximum(2 * c - far + slot, 0)
        return seg_ref[pl.ds(block, 1), :].astype(f32)

    seg_copy.wait()
    key_local = lax.broadcasted_iota(jnp.int32, (rows, rows), 0)
    query_local = lax.broadcasted_iota(jnp.int32, (rows, rows), 1)
    for slot in range(far + 2):
        key_seg = jnp.broadcast_to(seg_row(slot), (rows, rows)).T
        exists = 2 * c - far + slot >= 0
        for qi in range(2):
            at = slot - qi
            if 0 <= at < span:
                back = (far - at) * rows + query_local - key_local
                same = key_seg == jnp.broadcast_to(seg_row(far + qi), (rows, rows))
                allowed = (back >= 0) & (back < WINDOW) & same & exists
                bias[qi, pl.ds(at * rows, rows), :] = jnp.where(allowed, 0.0, masked_score)

    pieces = [(which, j) for which in range(2) for j in range(2)]

    def passed(which, g):
        if g == 0:
            return k >= 0
        skipped = (c % 4 == 3) | (which == 1)
        return (k == 0) | jnp.logical_not(skipped)

    def relay(g, part):
        @pl.when(odd & behind)
        def _():
            for which, j in part:
                kv_arrival(which, j, g).wait_recv()

                @pl.when(passed(which, g))
                def _():
                    pass_copy(which, j, g).start()

    def arrive(g, which):
        @pl.when(even & behind)
        def _():
            for j in range(2):
                kv_arrival(which, j, g).wait_recv()

        for copies in (own[g], swap[g]):
            for copy in copies[3:] if which else copies[:3]:
                copy.wait()

        @pl.when(c >= 1)
        def _():
            for j in range(2):
                kv_arrival(which, far - 2 + j, g).wait_recv()

    factor = DH**-0.5
    exponent = factor * math.log2(math.e)

    def stacked(ref, qi, g):
        return jnp.concatenate(
            [ref[g, qi, :, pl.ds(h * DH, DH)] for h in range(group)], axis=0
        )

    def keys(ref, qi, g):
        return ref[g, pl.ds(qi, span)].reshape(span * rows, DH)

    def nt(a, b):
        return lax.dot_general(a, b, (((1,), (1,)), ((), ())), preferred_element_type=f32)

    def grad_copy(d, j, g, which):
        return pltpu.make_async_remote_copy(
            src_ref=sbuf.at[far - 2 * d + j, g, which],
            dst_ref=rbuf.at[d - 1, k, g, which],
            send_sem=grad_send.at[d - 1, j, g, which],
            recv_sem=grad_recv.at[d - 1, k, g, which],
            device_id=dev(2 * (c - d) + j),
            device_id_type=MESH,
        )

    def mid_copy(j, g, which):
        return pltpu.make_async_remote_copy(
            src_ref=sbuf.at[far - 2 + j, g, which],
            dst_ref=mbuf.at[j, g, which],
            send_sem=grad_send.at[0, j, g, which],
            recv_sem=mid_recv.at[j, g, which],
            device_id=dev(2 * beside + k),
            device_id_type=MESH,
        )

    def grad_arrival(d, j, g, which):
        return pltpu.make_async_remote_copy(
            src_ref=sbuf.at[0, g, which],
            dst_ref=rbuf.at[d - 1, j, g, which],
            send_sem=grad_send.at[d - 1, 0, g, which],
            recv_sem=grad_recv.at[d - 1, j, g, which],
            device_id=dev(partner),
            device_id_type=MESH,
        )

    def part_copy(g):
        return pltpu.make_async_remote_copy(
            src_ref=pbuf.at[g, other],
            dst_ref=rpart.at[g],
            send_sem=gpart_send.at[g],
            recv_sem=gpart_recv.at[g],
            device_id=dev(partner),
            device_id_type=MESH,
        )

    def combine(g, which):
        @pl.when(odd & behind)
        def _():
            for j in range(2):
                mid_copy(j, g, which).wait_recv()
                total = acc[g, which, j] + mbuf[j, g, which].astype(f32)
                sbuf[j, g, which] = total.astype(bf16)
                grad_copy(2, j, g, which).start()

    def place(g, qi, which, part):
        for at in range(span):
            slot = at + qi
            piece = part[at * rows : (at + 1) * rows]
            if qi == 0 and slot > 0:
                acc[g, which, slot] = piece
                continue
            if qi == 1 and slot < far + 1:
                piece = acc[g, which, slot] + piece
            if slot < 2:
                acc[g, which, slot] = piece
            elif slot < far:
                sbuf[slot, g, which] = piece.astype(bf16)
            else:
                acc[g, which, slot] = piece
                pbuf[g, slot - far, which] = piece.astype(bf16)

    def send_even(g, which):
        @pl.when(even & behind)
        def _():
            for j in range(2):
                mid_copy(j, g, which).start()
            for j in range(2):
                sbuf[j, g, which] = acc[g, which, j].astype(bf16)

    def send_far(g, which):
        @pl.when(even & behind)
        def _():
            for j in range(2):
                grad_copy(2, j, g, which).start()

    for g in range(heads):
        if g == 0:
            relay(0, pieces)
        arrive(g, 0)
        if g == 1:
            combine(0, 1)
            send_far(0, 1)
            send_far(0, 0)
        for qi in range(2):
            q_rows, g_rows = stacked(qb, qi, g), stacked(gb, qi, g)
            mask = bias[qi]
            scores = nt(keys(kb, qi, g), q_rows) + jnp.concatenate([mask] * group, axis=1)
            top = jnp.max(scores, axis=0, keepdims=True)
            terms = jnp.exp2((scores - top) * exponent)
            inverse = 1.0 / jnp.sum(terms, axis=0, keepdims=True)
            prob = terms * inverse
            probs[qi] = prob
            dv = jnp.dot(prob.astype(bf16), g_rows, preferred_element_type=f32)
            place(g, qi, 1, dv)
        send_even(g, 1)
        if g == 1:
            send_far(1, 1)
        arrive(g, 1)
        for qi in range(2):
            q_rows, g_rows = stacked(qb, qi, g), stacked(gb, qi, g)
            prob = probs[qi]
            prob_grad = nt(keys(vb, qi, g), g_rows)
            delta = jnp.sum(prob * prob_grad, axis=0, keepdims=True)
            grad = (prob * (prob_grad - delta)).astype(bf16)
            dsb[g, qi] = grad
            dk = jnp.dot(grad, q_rows, preferred_element_type=f32) * factor
            place(g, qi, 0, dk)
        send_even(g, 0)
        if g == 1:
            send_far(1, 0)

        if g == 0:
            relay(1, pieces)

        @pl.when(odd)
        def _():
            for which in (1, 0):
                for j in range(2):
                    grad_copy(1, j, g, which).start()

        part_copy(g).start()

    combine(0, 0)
    for qi in range(2):
        for g in range(heads):
            dq = lax.dot_general(
                dsb[g, qi], keys(kb, qi, g), (((0,), (0,)), ((), ())), preferred_element_type=f32
            )
            dq = (dq * factor).astype(bf16)
            for h in range(group):
                dqb[qi, :, pl.ds((group * g + h) * DH, DH)] = dq[h * rows : (h + 1) * rows]
    dq_local = pltpu.make_async_copy(dqb.at[k], dq_out.at[0, :, cols(k, qhalf)], dq_sem.at[0])
    dq_local.start()
    dq_remote = pltpu.make_async_remote_copy(
        src_ref=dqb.at[other],
        dst_ref=dq_out.at[0, :, cols(k, qhalf)],
        send_sem=dq_sem.at[1],
        recv_sem=dq_sem.at[2],
        device_id=dev(partner),
        device_id_type=MESH,
    )
    dq_remote.start()
    combine(1, 1)
    combine(1, 0)

    for g in range(heads):
        part_copy(g).wait()
        for which, out in ((1, dv_out), (0, dk_out)):
            for d, ok in ((1, even), (2, ahead)):

                @pl.when(ok)
                def _():
                    for j in range(2):
                        grad_arrival(d, j, g, which).wait_recv()

            mine = acc[g, which, far + k]
            theirs = rpart[g, which].astype(f32)
            for d in range(reach):
                mine += rbuf[d, k, g, which].astype(f32)
                theirs += rbuf[d, other, g, which].astype(f32)
            out[0, :, cols(k * heads + g, DH)] = mine.astype(bf16)
            out[0, :, cols(other * heads + g, DH)] = theirs.astype(bf16)

    for d, ok in ((2, ahead), (1, even)):

        @pl.when(ok)
        def _():
            for g in range(heads):
                for which in range(2):
                    for j in range(2):
                        kv_copy(which, d, j, g).wait_send()

    @pl.when(odd & behind)
    def _():
        for g in range(heads):
            for which in range(2):

                @pl.when(passed(which, g))
                def _():
                    for j in range(2):
                        pass_copy(which, j, g).wait_send()

    for *_, copies, ok in direct:

        @pl.when(ok)
        def _():
            for head, core, which in copies:
                kv_copy(which, 1, core, head).wait_send()

    for d, ok in ((2, behind), (1, odd | behind)):

        @pl.when(ok)
        def _():
            for g in range(heads):
                for j in range(2):
                    for which in range(2):
                        grad_copy(d, j, g, which).wait_send()

    dq_local.wait()
    dq_remote.wait()


def local(queries, key_states, value_states, upstream, segments):
    count = lax.axis_size("ctx")
    sections = lax.axis_size("section")
    rows = queries.shape[1]
    out_grad = upstream
    if sections > 1:
        out_grad = lax.ppermute(
            upstream, "section", [(i, (i - 1) % sections) for i in range(sections)]
        )
    reach = -(-(WINDOW - 1) // (2 * rows))
    assert reach == 2 and count % 4 == 0
    far = 2 * reach
    span = far + 1
    heads = KVH // 2
    group = HQ // KVH
    qhalf = HQ // 2 * DH
    bf16, f32 = jnp.bfloat16, jnp.float32
    dma = pltpu.SemaphoreType.DMA
    hbm = pl.BlockSpec(memory_space=pltpu.HBM)
    vmem = pl.BlockSpec(memory_space=pltpu.VMEM)
    shapes = (
        jax.ShapeDtypeStruct(queries.shape, bf16),
        jax.ShapeDtypeStruct(key_states.shape, bf16),
        jax.ShapeDtypeStruct(value_states.shape, bf16),
    )
    operands = (queries, key_states, value_states, out_grad, segments.reshape(-1, rows))
    operands = [pltpu.with_memory_space_constraint(x, pltpu.HBM) for x in operands]
    results = pl.pallas_call(
        functools.partial(kernel, count, reach, rows),
        out_shape=shapes,
        in_specs=[hbm] * 5,
        out_specs=(vmem, vmem, vmem),
        scratch_shapes=[
            pltpu.VMEM((segments.shape[0] // rows, rows), jnp.int32),
            pltpu.VMEM((heads, 2, rows, group * DH), bf16),
            pltpu.VMEM((heads, 2, rows, group * DH), bf16),
            pltpu.VMEM((heads, far + 2, rows, DH), bf16),
            pltpu.VMEM((heads, far + 2, rows, DH), bf16),
            pltpu.VMEM((2, span * rows, rows), f32),
            pltpu.VMEM((heads, 2, span * rows, HQ // KVH * rows), bf16),
            pltpu.VMEM((heads, 2, far + 2, rows, DH), f32),
            pltpu.VMEM((2, span * rows, group * rows), f32),
            pltpu.VMEM((far, heads, 2, rows, DH), bf16),
            pltpu.VMEM((2, heads, 2, rows, DH), bf16),
            pltpu.VMEM((reach, 2, heads, 2, rows, DH), bf16),
            pltpu.VMEM((heads, 2, 2, rows, DH), bf16),
            pltpu.VMEM((heads, 2, rows, DH), bf16),
            pltpu.VMEM((2, rows, qhalf), bf16),
            dma((5, heads)),
            dma((4, heads)),
            dma((4, heads)),
            dma((2, reach, 2, heads)),
            dma((2, heads, far)),
            dma((2, 2, heads)),
            dma((reach, 2, heads, 2)),
            dma((reach, 2, heads, 2)),
            dma((2, heads, 2)),
            dma((heads,)),
            dma((heads,)),
            dma((3,)),
        ],
        compiler_params=pltpu.CompilerParams(
            collective_id=0, has_side_effects=True, vmem_limit_bytes=32 * 1024 * 1024
        ),
    )(*operands)
    return pl.pallas_call(
        emit,
        out_shape=shapes,
        in_specs=[pl.BlockSpec(memory_space=pl.ANY)] * 3,
        out_specs=[hbm] * 3,
        scratch_shapes=[dma((3,))],
        compiler_params=pltpu.CompilerParams(vmem_limit_bytes=1024 * 1024),
    )(*results)


def emit(a, b, c, a_out, b_out, c_out, sems):
    copies = [
        pltpu.make_async_copy(src, dst, sems.at[i])
        for i, (src, dst) in enumerate(((a, a_out), (b, b_out), (c, c_out)))
    ]
    for copy in copies:
        copy.start()
    for copy in copies:
        copy.wait()


def solution(mesh):
    split = P("section", "ctx", None)
    return jax.shard_map(
        local,
        mesh=mesh,
        in_specs=(split, split, split, split, P()),
        out_specs=(split, split, split),
        check_vma=False,
    )
```

```python
import functools
import math

import jax
import jax.numpy as jnp
from jax import lax
from jax.experimental import pallas as pl
from jax.experimental.pallas import tpu as pltpu
from jax.sharding import PartitionSpec as P

HQ = 8
KVH = 4
DH = 256
WINDOW = 512

MESH = pl.DeviceIdType.MESH
masked_score = -1e30


def kernel(
    count, reach, rows,
    q_in, k_in, v_in, g_in, seg_in,
    dq_out, dk_out, dv_out,
    seg_ref, qb, gb, kb, vb, bias, dsb, acc, probs, sbuf, mbuf, rbuf, pbuf, rpart, dqb,
    local_sem, part_send, part_recv, kv_send, kv_recv, pass_send,
    grad_send, grad_recv, mid_recv, gpart_send, gpart_recv, dq_sem,
):
    bf16, f32 = jnp.bfloat16, jnp.float32
    pairs = count // 2
    far = 2 * reach
    span = far + 1
    heads = KVH // 2
    qhalf = HQ // 2 * DH
    group = HQ // KVH
    me = lax.axis_index("ctx")
    c = me // 2
    k = me % 2
    other = 1 - k
    partner = 2 * c + other
    odd = c % 2 == 1
    even = c % 2 == 0
    beside = c + 1 - 2 * (c % 2)
    behind = c >= 2
    ahead = c + 2 < pairs
    hop = odd & (c + 1 < pairs)
    direct = [(0, 0, [(1, 1, 0), (1, 1, 1)], hop & (c % 4 == 1)), (1, 0, [(1, 1, 1)], hop & (c % 4 == 3))]

    def dev(index):
        return {"ctx": index}

    def cols(index, width):
        return pl.ds(pl.multiple_of(index * width, width), width)

    barrier = pltpu.get_barrier_semaphore()
    pl.semaphore_signal(barrier, inc=1, device_id=dev(partner), device_id_type=MESH)
    for j in range(2):
        pl.semaphore_signal(
            barrier, inc=1, device_id=dev(2 * beside + j), device_id_type=MESH
        )
    for there, ok in ((c - 2, behind), (c + 2, ahead)):

        @pl.when(ok)
        def _():
            for j in range(2):
                pl.semaphore_signal(
                    barrier, inc=1, device_id=dev(2 * there + j), device_id_type=MESH
                )

    @pl.when(even & (c >= 1) & (k == 1))
    def _():
        for j in range(2):
            pl.semaphore_signal(
                barrier, inc=1, device_id=dev(2 * (c - 1) + j), device_id_type=MESH
            )

    greeted = 3 + jnp.where(behind, 2, 0) + jnp.where(ahead, 2, 0) + jnp.where(hop, 1, 0)

    def kv_copy(which, d, j, g):
        src, dst = ((k_in, kb), (v_in, vb))[which]
        slot = far - 2 * d + k
        return pltpu.make_async_remote_copy(
            src_ref=src.at[0, :, pl.ds((j * heads + g) * DH, DH)],
            dst_ref=dst.at[g, slot],
            send_sem=kv_send.at[which, d - 1, j, g],
            recv_sem=kv_recv.at[which, g, slot],
            device_id=dev(2 * (c + d) + j),
            device_id_type=MESH,
        )

    def kv_arrival(which, slot, g):
        src, dst = ((k_in, kb), (v_in, vb))[which]
        return pltpu.make_async_remote_copy(
            src_ref=src.at[0, :, pl.ds(0, DH)],
            dst_ref=dst.at[g, slot],
            send_sem=kv_send.at[which, 0, 0, g],
            recv_sem=kv_recv.at[which, g, slot],
            device_id=dev(partner),
            device_id_type=MESH,
        )

    def pass_copy(which, j, g):
        ref = (kb, vb)[which]
        return pltpu.make_async_remote_copy(
            src_ref=ref.at[g, j],
            dst_ref=ref.at[g, far - 2 + j],
            send_sem=pass_send.at[which, j, g],
            recv_sem=kv_recv.at[which, g, far - 2 + j],
            device_id=dev(2 * beside + k),
            device_id_type=MESH,
        )

    seg_copy = pltpu.make_async_copy(seg_in, seg_ref, local_sem.at[4, 0])
    seg_copy.start()
    swaps = ((q_in, qb, group * DH, 0), (g_in, gb, group * DH, 0), (k_in, kb, DH, far), (v_in, vb, DH, far))
    own = [
        [
            pltpu.make_async_copy(
                src.at[0, :, cols(k * heads + g, width)], dst.at[g, base + k], local_sem.at[i, g]
            )
            for i, (src, dst, width, base) in enumerate(swaps)
        ]
        for g in range(heads)
    ]
    for copy in own[0] + own[1]:
        copy.start()

    @pl.when(c < 2)
    def _():
        for slot in range(2):
            kb[:, slot] = jnp.zeros((heads, rows, DH), bf16)
            vb[:, slot] = jnp.zeros((heads, rows, DH), bf16)

    @pl.when(c == 0)
    def _():
        for slot in range(2, far):
            kb[:, slot] = jnp.zeros((heads, rows, DH), bf16)
            vb[:, slot] = jnp.zeros((heads, rows, DH), bf16)

    @pl.when(odd)
    def _():
        rbuf[0] = jnp.zeros(rbuf.shape[1:], bf16)

    @pl.when(c + 2 >= pairs)
    def _():
        rbuf[1] = jnp.zeros(rbuf.shape[1:], bf16)

    pl.semaphore_wait(barrier, greeted)

    swap = [
        [
            pltpu.make_async_remote_copy(
                src_ref=src.at[0, :, cols(other * heads + g, width)],
                dst_ref=dst.at[g, base + k],
                send_sem=part_send.at[i, g],
                recv_sem=part_recv.at[i, g],
                device_id=dev(partner),
                device_id_type=MESH,
            )
            for i, (src, dst, width, base) in enumerate(swaps)
        ]
        for g in range(heads)
    ]
    for g in range(heads):
        for j in range(2):
            for which in range(2):
                for d, ok in ((2, ahead), (1, even)):

                    @pl.when(ok)
                    def _():
                        kv_copy(which, d, j, g).start()

            for *after, copies, ok in direct:
                if after == [g, j]:

                    @pl.when(ok)
                    def _():
                        for head, core, which in copies:
                            kv_copy(which, 1, core, head).start()

        for copy in swap[g]:
            copy.start()

    def seg_row(slot):
        block = jnp.maximum(2 * c - far + slot, 0)
        return seg_ref[pl.ds(block, 1), :].astype(f32)

    seg_copy.wait()
    key_local = lax.broadcasted_iota(jnp.int32, (rows, rows), 0)
    query_local = lax.broadcasted_iota(jnp.int32, (rows, rows), 1)
    for slot in range(far + 2):
        key_seg = jnp.broadcast_to(seg_row(slot), (rows, rows)).T
        exists = 2 * c - far + slot >= 0
        for qi in range(2):
            at = slot - qi
            if 0 <= at < span:
                back = (far - at) * rows + query_local - key_local
                same = key_seg == jnp.broadcast_to(seg_row(far + qi), (rows, rows))
                allowed = (back >= 0) & (back < WINDOW) & same & exists
                bias[qi, pl.ds(at * rows, rows), :] = jnp.where(allowed, 0.0, masked_score)

    pieces = [(which, j) for which in range(2) for j in range(2)]

    def passed(which, g):
        if g == 0:
            return k >= 0
        skipped = (c % 4 == 3) | (which == 1)
        return (k == 0) | jnp.logical_not(skipped)

    def relay(g, part):
        @pl.when(odd & behind)
        def _():
            for which, j in part:
                kv_arrival(which, j, g).wait_recv()

                @pl.when(passed(which, g))
                def _():
                    pass_copy(which, j, g).start()

    def arrive(g, which):
        @pl.when(even & behind)
        def _():
            for j in range(2):
                kv_arrival(which, j, g).wait_recv()

        for copies in (own[g], swap[g]):
            for copy in copies[3:] if which else copies[:3]:
                copy.wait()

        @pl.when(c >= 1)
        def _():
            for j in range(2):
                kv_arrival(which, far - 2 + j, g).wait_recv()

    factor = DH**-0.5
    exponent = factor * math.log2(math.e)

    def stacked(ref, qi, g):
        return jnp.concatenate(
            [ref[g, qi, :, pl.ds(h * DH, DH)] for h in range(group)], axis=0
        )

    def keys(ref, qi, g):
        return ref[g, pl.ds(qi, span)].reshape(span * rows, DH)

    def nt(a, b):
        return lax.dot_general(a, b, (((1,), (1,)), ((), ())), preferred_element_type=f32)

    def grad_copy(d, j, g, which):
        return pltpu.make_async_remote_copy(
            src_ref=sbuf.at[far - 2 * d + j, g, which],
            dst_ref=rbuf.at[d - 1, k, g, which],
            send_sem=grad_send.at[d - 1, j, g, which],
            recv_sem=grad_recv.at[d - 1, k, g, which],
            device_id=dev(2 * (c - d) + j),
            device_id_type=MESH,
        )

    def mid_copy(j, g, which):
        return pltpu.make_async_remote_copy(
            src_ref=sbuf.at[far - 2 + j, g, which],
            dst_ref=mbuf.at[j, g, which],
            send_sem=grad_send.at[0, j, g, which],
            recv_sem=mid_recv.at[j, g, which],
            device_id=dev(2 * beside + k),
            device_id_type=MESH,
        )

    def grad_arrival(d, j, g, which):
        return pltpu.make_async_remote_copy(
            src_ref=sbuf.at[0, g, which],
            dst_ref=rbuf.at[d - 1, j, g, which],
            send_sem=grad_send.at[d - 1, 0, g, which],
            recv_sem=grad_recv.at[d - 1, j, g, which],
            device_id=dev(partner),
            device_id_type=MESH,
        )

    def part_copy(g):
        return pltpu.make_async_remote_copy(
            src_ref=pbuf.at[g, other],
            dst_ref=rpart.at[g],
            send_sem=gpart_send.at[g],
            recv_sem=gpart_recv.at[g],
            device_id=dev(partner),
            device_id_type=MESH,
        )

    def combine(g, which):
        @pl.when(odd & behind)
        def _():
            for j in range(2):
                mid_copy(j, g, which).wait_recv()
                total = acc[g, which, j] + mbuf[j, g, which].astype(f32)
                sbuf[j, g, which] = total.astype(bf16)
                grad_copy(2, j, g, which).start()

    def place(g, qi, which, part):
        for at in range(span):
            slot = at + qi
            piece = part[at * rows : (at + 1) * rows]
            if qi == 0 and slot > 0:
                acc[g, which, slot] = piece
                continue
            if qi == 1 and slot < far + 1:
                piece = acc[g, which, slot] + piece
            if slot < 2:
                acc[g, which, slot] = piece
            elif slot < far:
                sbuf[slot, g, which] = piece.astype(bf16)
            else:
                acc[g, which, slot] = piece
                pbuf[g, slot - far, which] = piece.astype(bf16)

    def send_even(g, which):
        @pl.when(even & behind)
        def _():
            for j in range(2):
                mid_copy(j, g, which).start()
            for j in range(2):
                sbuf[j, g, which] = acc[g, which, j].astype(bf16)

    low = c % 4 == 0
    high = c % 4 == 2
    every = c >= 0
    far_plan = [(0, 1, 1, high), (0, 0, 2, high), (0, 1, 2, low), (0, 0, 2, low), (1, 1, 3, every), (1, 0, 4, every)]

    def send_far(point):
        for g, which, when, ok in far_plan:
            if when == point:

                @pl.when(even & behind & ok)
                def _():
                    for j in range(2):
                        grad_copy(2, j, g, which).start()

    for g in range(heads):
        if g == 0:
            relay(0, pieces)
        arrive(g, 0)
        if g == 1:
            combine(0, 1)
            send_far(2)
        for qi in range(2):
            q_rows, g_rows = stacked(qb, qi, g), stacked(gb, qi, g)
            mask = bias[qi]
            scores = nt(keys(kb, qi, g), q_rows) + jnp.concatenate([mask] * group, axis=1)
            top = jnp.max(scores, axis=0, keepdims=True)
            terms = jnp.exp2((scores - top) * exponent)
            inverse = 1.0 / jnp.sum(terms, axis=0, keepdims=True)
            prob = terms * inverse
            probs[qi] = prob
            dv = jnp.dot(prob.astype(bf16), g_rows, preferred_element_type=f32)
            place(g, qi, 1, dv)
        send_even(g, 1)
        send_far(3 * g)
        arrive(g, 1)
        for qi in range(2):
            q_rows, g_rows = stacked(qb, qi, g), stacked(gb, qi, g)
            prob = probs[qi]
            prob_grad = nt(keys(vb, qi, g), g_rows)
            delta = jnp.sum(prob * prob_grad, axis=0, keepdims=True)
            grad = (prob * (prob_grad - delta)).astype(bf16)
            dsb[g, qi] = grad
            dk = jnp.dot(grad, q_rows, preferred_element_type=f32) * factor
            place(g, qi, 0, dk)
        send_even(g, 0)
        send_far(3 * g + 1)

        if g == 0:
            relay(1, pieces)

        @pl.when(odd)
        def _():
            for which in (1, 0):
                for j in range(2):
                    grad_copy(1, j, g, which).start()

        part_copy(g).start()

    combine(0, 0)
    for qi in range(2):
        for g in range(heads):
            dq = lax.dot_general(
                dsb[g, qi], keys(kb, qi, g), (((0,), (0,)), ((), ())), preferred_element_type=f32
            )
            dq = (dq * factor).astype(bf16)
            for h in range(group):
                dqb[qi, :, pl.ds((group * g + h) * DH, DH)] = dq[h * rows : (h + 1) * rows]
    dq_local = pltpu.make_async_copy(dqb.at[k], dq_out.at[0, :, cols(k, qhalf)], dq_sem.at[0])
    dq_local.start()
    dq_remote = pltpu.make_async_remote_copy(
        src_ref=dqb.at[other],
        dst_ref=dq_out.at[0, :, cols(k, qhalf)],
        send_sem=dq_sem.at[1],
        recv_sem=dq_sem.at[2],
        device_id=dev(partner),
        device_id_type=MESH,
    )
    dq_remote.start()
    combine(1, 1)
    combine(1, 0)

    for g in range(heads):
        part_copy(g).wait()
        for which, out in ((1, dv_out), (0, dk_out)):
            for d, ok in ((1, even), (2, ahead)):

                @pl.when(ok)
                def _():
                    for j in range(2):
                        grad_arrival(d, j, g, which).wait_recv()

            mine = acc[g, which, far + k]
            theirs = rpart[g, which].astype(f32)
            for d in range(reach):
                mine += rbuf[d, k, g, which].astype(f32)
                theirs += rbuf[d, other, g, which].astype(f32)
            out[0, :, cols(k * heads + g, DH)] = mine.astype(bf16)
            out[0, :, cols(other * heads + g, DH)] = theirs.astype(bf16)

    for d, ok in ((2, ahead), (1, even)):

        @pl.when(ok)
        def _():
            for g in range(heads):
                for which in range(2):
                    for j in range(2):
                        kv_copy(which, d, j, g).wait_send()

    @pl.when(odd & behind)
    def _():
        for g in range(heads):
            for which in range(2):

                @pl.when(passed(which, g))
                def _():
                    for j in range(2):
                        pass_copy(which, j, g).wait_send()

    for *_, copies, ok in direct:

        @pl.when(ok)
        def _():
            for head, core, which in copies:
                kv_copy(which, 1, core, head).wait_send()

    for d, ok in ((2, behind), (1, odd | behind)):

        @pl.when(ok)
        def _():
            for g in range(heads):
                for j in range(2):
                    for which in range(2):
                        grad_copy(d, j, g, which).wait_send()

    dq_local.wait()
    dq_remote.wait()


def local(queries, key_states, value_states, upstream, segments):
    count = lax.axis_size("ctx")
    sections = lax.axis_size("section")
    rows = queries.shape[1]
    out_grad = upstream
    if sections > 1:
        out_grad = lax.ppermute(
            upstream, "section", [(i, (i - 1) % sections) for i in range(sections)]
        )
    reach = -(-(WINDOW - 1) // (2 * rows))
    assert reach == 2 and count % 4 == 0
    far = 2 * reach
    span = far + 1
    heads = KVH // 2
    group = HQ // KVH
    qhalf = HQ // 2 * DH
    bf16, f32 = jnp.bfloat16, jnp.float32
    dma = pltpu.SemaphoreType.DMA
    hbm = pl.BlockSpec(memory_space=pltpu.HBM)
    vmem = pl.BlockSpec(memory_space=pltpu.VMEM)
    shapes = (
        jax.ShapeDtypeStruct(queries.shape, bf16),
        jax.ShapeDtypeStruct(key_states.shape, bf16),
        jax.ShapeDtypeStruct(value_states.shape, bf16),
    )
    operands = (queries, key_states, value_states, out_grad, segments.reshape(-1, rows))
    operands = [pltpu.with_memory_space_constraint(x, pltpu.HBM) for x in operands]
    results = pl.pallas_call(
        functools.partial(kernel, count, reach, rows),
        out_shape=shapes,
        in_specs=[hbm] * 5,
        out_specs=(vmem, vmem, vmem),
        scratch_shapes=[
            pltpu.VMEM((segments.shape[0] // rows, rows), jnp.int32),
            pltpu.VMEM((heads, 2, rows, group * DH), bf16),
            pltpu.VMEM((heads, 2, rows, group * DH), bf16),
            pltpu.VMEM((heads, far + 2, rows, DH), bf16),
            pltpu.VMEM((heads, far + 2, rows, DH), bf16),
            pltpu.VMEM((2, span * rows, rows), f32),
            pltpu.VMEM((heads, 2, span * rows, HQ // KVH * rows), bf16),
            pltpu.VMEM((heads, 2, far + 2, rows, DH), f32),
            pltpu.VMEM((2, span * rows, group * rows), f32),
            pltpu.VMEM((far, heads, 2, rows, DH), bf16),
            pltpu.VMEM((2, heads, 2, rows, DH), bf16),
            pltpu.VMEM((reach, 2, heads, 2, rows, DH), bf16),
            pltpu.VMEM((heads, 2, 2, rows, DH), bf16),
            pltpu.VMEM((heads, 2, rows, DH), bf16),
            pltpu.VMEM((2, rows, qhalf), bf16),
            dma((5, heads)),
            dma((4, heads)),
            dma((4, heads)),
            dma((2, reach, 2, heads)),
            dma((2, heads, far)),
            dma((2, 2, heads)),
            dma((reach, 2, heads, 2)),
            dma((reach, 2, heads, 2)),
            dma((2, heads, 2)),
            dma((heads,)),
            dma((heads,)),
            dma((3,)),
        ],
        compiler_params=pltpu.CompilerParams(
            collective_id=0, has_side_effects=True, vmem_limit_bytes=32 * 1024 * 1024
        ),
    )(*operands)
    return pl.pallas_call(
        emit,
        out_shape=shapes,
        in_specs=[pl.BlockSpec(memory_space=pl.ANY)] * 3,
        out_specs=[hbm] * 3,
        scratch_shapes=[dma((3,))],
        compiler_params=pltpu.CompilerParams(vmem_limit_bytes=1024 * 1024),
    )(*results)


def emit(a, b, c, a_out, b_out, c_out, sems):
    copies = [
        pltpu.make_async_copy(src, dst, sems.at[i])
        for i, (src, dst) in enumerate(((a, a_out), (b, b_out), (c, c_out)))
    ]
    for copy in copies:
        copy.start()
    for copy in copies:
        copy.wait()


def solution(mesh):
    split = P("section", "ctx", None)
    return jax.shard_map(
        local,
        mesh=mesh,
        in_specs=(split, split, split, split, P()),
        out_specs=(split, split, split),
        check_vma=False,
    )
```

```python
import functools
import math

import jax
import jax.numpy as jnp
from jax import lax
from jax.experimental import pallas as pl
from jax.experimental.pallas import tpu as pltpu
from jax.sharding import PartitionSpec as P

HQ = 8
KVH = 4
DH = 256
WINDOW = 512

MESH = pl.DeviceIdType.MESH
masked_score = -1e30


def kernel(
    count, reach, rows,
    q_in, k_in, v_in, g_in, seg_in,
    dq_out, dk_out, dv_out,
    seg_ref, qb, gb, kb, vb, bias, dsb, acc, probs, sbuf, mbuf, rbuf, pbuf, rpart, dqb,
    local_sem, part_send, part_recv, kv_send, kv_recv, pass_send,
    grad_send, grad_recv, mid_recv, gpart_send, gpart_recv, dq_sem,
):
    bf16, f32 = jnp.bfloat16, jnp.float32
    pairs = count // 2
    far = 2 * reach
    span = far + 1
    heads = KVH // 2
    qhalf = HQ // 2 * DH
    group = HQ // KVH
    me = lax.axis_index("ctx")
    c = me // 2
    k = me % 2
    other = 1 - k
    partner = 2 * c + other
    odd = c % 2 == 1
    even = c % 2 == 0
    beside = c + 1 - 2 * (c % 2)
    behind = c >= 2
    ahead = c + 2 < pairs
    hop = odd & (c + 1 < pairs)
    direct = [(0, 0, [(1, 1, 0), (1, 1, 1)], hop & (c % 4 == 1)), (1, 0, [(1, 1, 1)], hop & (c % 4 == 3))]

    def dev(index):
        return {"ctx": index}

    def cols(index, width):
        return pl.ds(pl.multiple_of(index * width, width), width)

    barrier = pltpu.get_barrier_semaphore()
    pl.semaphore_signal(barrier, inc=1, device_id=dev(partner), device_id_type=MESH)
    for j in range(2):
        pl.semaphore_signal(
            barrier, inc=1, device_id=dev(2 * beside + j), device_id_type=MESH
        )
    for there, ok in ((c - 2, behind), (c + 2, ahead)):

        @pl.when(ok)
        def _():
            for j in range(2):
                pl.semaphore_signal(
                    barrier, inc=1, device_id=dev(2 * there + j), device_id_type=MESH
                )

    @pl.when(even & (c >= 1) & (k == 1))
    def _():
        for j in range(2):
            pl.semaphore_signal(
                barrier, inc=1, device_id=dev(2 * (c - 1) + j), device_id_type=MESH
            )

    greeted = 3 + jnp.where(behind, 2, 0) + jnp.where(ahead, 2, 0) + jnp.where(hop, 1, 0)

    def blocks(number):
        return {
            1: sbuf.at[0, 0, 0], 2: sbuf.at[0, 0], 4: sbuf.at[0], 8: sbuf.at[pl.ds(0, 2)]
        }[number]

    def sent(sem, ref):
        pltpu.make_async_remote_copy(
            src_ref=ref, dst_ref=ref, send_sem=sem, recv_sem=sem,
            device_id=dev(partner), device_id_type=MESH,
        ).wait_send()

    def landed(sem, ref):
        pltpu.make_async_remote_copy(
            src_ref=ref, dst_ref=ref, send_sem=sem, recv_sem=sem,
            device_id=dev(partner), device_id_type=MESH,
        ).wait_recv()

    def kv_copy(which, d, j, g):
        src, dst = ((k_in, kb), (v_in, vb))[which]
        return pltpu.make_async_remote_copy(
            src_ref=src.at[0, :, pl.ds((j * heads + g) * DH, DH)],
            dst_ref=dst.at[g, far - 2 * d + k],
            send_sem=kv_send.at[d - 1],
            recv_sem=kv_recv.at[which, g, d - 1],
            device_id=dev(2 * (c + d) + j),
            device_id_type=MESH,
        )

    def kv_landed(which, d, g):
        landed(kv_recv.at[which, g, d - 1], (kb, vb)[which].at[g, pl.ds(far - 2 * d, 2)])

    def pass_copy(which, g):
        ref = (kb, vb)[which]
        return pltpu.make_async_remote_copy(
            src_ref=ref.at[g, pl.ds(0, 2)],
            dst_ref=ref.at[g, pl.ds(far - 2, 2)],
            send_sem=pass_send.at[which, g],
            recv_sem=kv_recv.at[which, g, 0],
            device_id=dev(2 * beside + k),
            device_id_type=MESH,
        )

    seg_copy = pltpu.make_async_copy(seg_in, seg_ref, local_sem.at[heads, 0])
    seg_copy.start()
    swaps = ((q_in, qb, group * DH, 0), (g_in, gb, group * DH, 0), (k_in, kb, DH, far), (v_in, vb, DH, far))
    own = [
        [
            pltpu.make_async_copy(
                src.at[0, :, cols(k * heads + g, width)], dst.at[g, base + k], local_sem.at[g, i // 3]
            )
            for i, (src, dst, width, base) in enumerate(swaps)
        ]
        for g in range(heads)
    ]
    for copy in own[0] + own[1]:
        copy.start()

    @pl.when(c < 2)
    def _():
        for slot in range(2):
            kb[:, slot] = jnp.zeros((heads, rows, DH), bf16)
            vb[:, slot] = jnp.zeros((heads, rows, DH), bf16)

    @pl.when(c == 0)
    def _():
        for slot in range(2, far):
            kb[:, slot] = jnp.zeros((heads, rows, DH), bf16)
            vb[:, slot] = jnp.zeros((heads, rows, DH), bf16)

    @pl.when(odd)
    def _():
        rbuf[0] = jnp.zeros(rbuf.shape[1:], bf16)

    @pl.when(c + 2 >= pairs)
    def _():
        rbuf[1] = jnp.zeros(rbuf.shape[1:], bf16)

    pl.semaphore_wait(barrier, greeted)

    swap = [
        [
            pltpu.make_async_remote_copy(
                src_ref=src.at[0, :, cols(other * heads + g, width)],
                dst_ref=dst.at[g, base + k],
                send_sem=part_send.at[0],
                recv_sem=part_recv.at[g, i // 3],
                device_id=dev(partner),
                device_id_type=MESH,
            )
            for i, (src, dst, width, base) in enumerate(swaps)
        ]
        for g in range(heads)
    ]
    for g in range(heads):
        for j in range(2):
            for which in range(2):
                for d, ok in ((2, ahead), (1, even)):

                    @pl.when(ok)
                    def _():
                        kv_copy(which, d, j, g).start()

            for *after, copies, ok in direct:
                if after == [g, j]:

                    @pl.when(ok)
                    def _():
                        for head, core, which in copies:
                            kv_copy(which, 1, core, head).start()

        for copy in swap[g]:
            copy.start()

    def seg_row(slot):
        block = jnp.maximum(2 * c - far + slot, 0)
        return seg_ref[pl.ds(block, 1), :].astype(f32)

    seg_copy.wait()
    key_local = lax.broadcasted_iota(jnp.int32, (rows, rows), 0)
    query_local = lax.broadcasted_iota(jnp.int32, (rows, rows), 1)
    for slot in range(far + 2):
        key_seg = jnp.broadcast_to(seg_row(slot), (rows, rows)).T
        exists = 2 * c - far + slot >= 0
        for qi in range(2):
            at = slot - qi
            if 0 <= at < span:
                back = (far - at) * rows + query_local - key_local
                same = key_seg == jnp.broadcast_to(seg_row(far + qi), (rows, rows))
                allowed = (back >= 0) & (back < WINDOW) & same & exists
                bias[qi, pl.ds(at * rows, rows), :] = jnp.where(allowed, 0.0, masked_score)

    def passed(which, g):
        if g == 0:
            return k >= 0
        skipped = (c % 4 == 3) | (which == 1)
        return (k == 0) | jnp.logical_not(skipped)

    def relay(g):
        @pl.when(odd & behind)
        def _():
            for which in range(2):
                kv_landed(which, 2, g)

                @pl.when(passed(which, g))
                def _():
                    pass_copy(which, g).start()

    def arrive(g, which):
        @pl.when(even & behind)
        def _():
            kv_landed(which, 2, g)

        exchanged = kb.at[0, 0] if which else kb.at[0, pl.ds(0, 2 * group + 1)]
        pltpu.make_async_copy(exchanged, exchanged, local_sem.at[g, which]).wait()
        landed(part_recv.at[g, which], exchanged)

        @pl.when(c >= 1)
        def _():
            kv_landed(which, 1, g)

    factor = DH**-0.5
    exponent = factor * math.log2(math.e)

    def stacked(ref, qi, g):
        return jnp.concatenate(
            [ref[g, qi, :, pl.ds(h * DH, DH)] for h in range(group)], axis=0
        )

    def keys(ref, qi, g):
        return ref[g, pl.ds(qi, span)].reshape(span * rows, DH)

    def nt(a, b):
        return lax.dot_general(a, b, (((1,), (1,)), ((), ())), preferred_element_type=f32)

    def grad_copy(d, j, g, which):
        return pltpu.make_async_remote_copy(
            src_ref=sbuf.at[far - 2 * d + j, g, which],
            dst_ref=rbuf.at[d - 1, k, g, which],
            send_sem=grad_send.at[d - 1],
            recv_sem=grad_recv.at[d - 1, g, which],
            device_id=dev(2 * (c - d) + j),
            device_id_type=MESH,
        )

    def mid_copy(j, g, which):
        return pltpu.make_async_remote_copy(
            src_ref=sbuf.at[far - 2 + j, g, which],
            dst_ref=mbuf.at[j, g, which],
            send_sem=grad_send.at[0],
            recv_sem=mid_recv.at[j, g, which],
            device_id=dev(2 * beside + k),
            device_id_type=MESH,
        )

    def part_copy(g):
        return pltpu.make_async_remote_copy(
            src_ref=pbuf.at[g, other],
            dst_ref=rpart.at[g],
            send_sem=gpart_send.at[g],
            recv_sem=gpart_recv.at[g],
            device_id=dev(partner),
            device_id_type=MESH,
        )

    def combine(g, which):
        @pl.when(odd & behind)
        def _():
            for j in range(2):
                mid_copy(j, g, which).wait_recv()
                total = acc[g, which, j] + mbuf[j, g, which].astype(f32)
                sbuf[j, g, which] = total.astype(bf16)
                grad_copy(2, j, g, which).start()

    def place(g, qi, which, part):
        for at in range(span):
            slot = at + qi
            piece = part[at * rows : (at + 1) * rows]
            if qi == 0 and slot > 0:
                acc[g, which, slot] = piece
                continue
            if qi == 1 and slot < far + 1:
                piece = acc[g, which, slot] + piece
            if slot < 2:
                acc[g, which, slot] = piece
            elif slot < far:
                sbuf[slot, g, which] = piece.astype(bf16)
            else:
                acc[g, which, slot] = piece
                pbuf[g, slot - far, which] = piece.astype(bf16)

    def send_even(g, which):
        @pl.when(even & behind)
        def _():
            for j in range(2):
                mid_copy(j, g, which).start()
            for j in range(2):
                sbuf[j, g, which] = acc[g, which, j].astype(bf16)

    low = c % 4 == 0
    high = c % 4 == 2
    every = c >= 0
    far_plan = [(0, 1, 1, high), (0, 0, 2, high), (0, 1, 2, low), (0, 0, 2, low), (1, 1, 3, every), (1, 0, 4, every)]

    def send_far(point):
        for g, which, when, ok in far_plan:
            if when == point:

                @pl.when(even & behind & ok)
                def _():
                    for j in range(2):
                        grad_copy(2, j, g, which).start()

    for g in range(heads):
        if g == 0:
            relay(0)
        arrive(g, 0)
        if g == 1:
            combine(0, 1)
            send_far(2)
        for qi in range(2):
            q_rows, g_rows = stacked(qb, qi, g), stacked(gb, qi, g)
            mask = bias[qi]
            scores = nt(keys(kb, qi, g), q_rows) + jnp.concatenate([mask] * group, axis=1)
            top = jnp.max(scores, axis=0, keepdims=True)
            terms = jnp.exp2((scores - top) * exponent)
            inverse = 1.0 / jnp.sum(terms, axis=0, keepdims=True)
            prob = terms * inverse
            probs[qi] = prob
            dv = jnp.dot(prob.astype(bf16), g_rows, preferred_element_type=f32)
            place(g, qi, 1, dv)
        send_even(g, 1)
        send_far(3 * g)
        arrive(g, 1)
        for qi in range(2):
            q_rows, g_rows = stacked(qb, qi, g), stacked(gb, qi, g)
            prob = probs[qi]
            prob_grad = nt(keys(vb, qi, g), g_rows)
            delta = jnp.sum(prob * prob_grad, axis=0, keepdims=True)
            grad = (prob * (prob_grad - delta)).astype(bf16)
            dsb[g, qi] = grad
            dk = jnp.dot(grad, q_rows, preferred_element_type=f32) * factor
            place(g, qi, 0, dk)
        send_even(g, 0)
        send_far(3 * g + 1)

        if g == 0:
            relay(1)

        @pl.when(odd)
        def _():
            for which in (1, 0):
                for j in range(2):
                    grad_copy(1, j, g, which).start()

        part_copy(g).start()

    combine(0, 0)
    for qi in range(2):
        for g in range(heads):
            dq = lax.dot_general(
                dsb[g, qi], keys(kb, qi, g), (((0,), (0,)), ((), ())), preferred_element_type=f32
            )
            dq = (dq * factor).astype(bf16)
            for h in range(group):
                dqb[qi, :, pl.ds((group * g + h) * DH, DH)] = dq[h * rows : (h + 1) * rows]
    dq_local = pltpu.make_async_copy(dqb.at[k], dq_out.at[0, :, cols(k, qhalf)], dq_sem.at[0])
    dq_local.start()
    dq_remote = pltpu.make_async_remote_copy(
        src_ref=dqb.at[other],
        dst_ref=dq_out.at[0, :, cols(k, qhalf)],
        send_sem=dq_sem.at[1],
        recv_sem=dq_sem.at[2],
        device_id=dev(partner),
        device_id_type=MESH,
    )
    dq_remote.start()
    combine(1, 1)
    combine(1, 0)

    for g in range(heads):
        part_copy(g).wait()
        for which, out in ((1, dv_out), (0, dk_out)):
            for d, ok in ((1, even), (2, ahead)):

                @pl.when(ok)
                def _():
                    landed(grad_recv.at[d - 1, g, which], rbuf.at[d - 1, :, g, which])

            mine = acc[g, which, far + k]
            theirs = rpart[g, which].astype(f32)
            for d in range(reach):
                mine += rbuf[d, k, g, which].astype(f32)
                theirs += rbuf[d, other, g, which].astype(f32)
            out[0, :, cols(k * heads + g, DH)] = mine.astype(bf16)
            out[0, :, cols(other * heads + g, DH)] = theirs.astype(bf16)

    sent(part_send.at[0], kb)
    for d, ok in ((2, ahead), (1, even)):

        @pl.when(ok)
        def _():
            sent(kv_send.at[d - 1], blocks(8))

    for *_, copies, ok in direct:

        @pl.when(ok)
        def _():
            sent(kv_send.at[0], blocks(len(copies)))

    @pl.when(odd & behind)
    def _():
        for g in range(heads):
            for which in range(2):

                @pl.when(passed(which, g))
                def _():
                    pass_copy(which, g).wait_send()

    for d, ok in ((2, behind), (1, odd | behind)):

        @pl.when(ok)
        def _():
            sent(grad_send.at[d - 1], blocks(8))

    dq_local.wait()
    dq_remote.wait()


def local(queries, key_states, value_states, upstream, segments):
    count = lax.axis_size("ctx")
    sections = lax.axis_size("section")
    rows = queries.shape[1]
    out_grad = upstream
    if sections > 1:
        out_grad = lax.ppermute(
            upstream, "section", [(i, (i - 1) % sections) for i in range(sections)]
        )
    reach = -(-(WINDOW - 1) // (2 * rows))
    assert reach == 2 and count % 4 == 0
    far = 2 * reach
    span = far + 1
    heads = KVH // 2
    group = HQ // KVH
    qhalf = HQ // 2 * DH
    bf16, f32 = jnp.bfloat16, jnp.float32
    dma = pltpu.SemaphoreType.DMA
    hbm = pl.BlockSpec(memory_space=pltpu.HBM)
    vmem = pl.BlockSpec(memory_space=pltpu.VMEM)
    shapes = (
        jax.ShapeDtypeStruct(queries.shape, bf16),
        jax.ShapeDtypeStruct(key_states.shape, bf16),
        jax.ShapeDtypeStruct(value_states.shape, bf16),
    )
    operands = (queries, key_states, value_states, out_grad, segments.reshape(-1, rows))
    operands = [pltpu.with_memory_space_constraint(x, pltpu.HBM) for x in operands]
    results = pl.pallas_call(
        functools.partial(kernel, count, reach, rows),
        out_shape=shapes,
        in_specs=[hbm] * 5,
        out_specs=(vmem, vmem, vmem),
        scratch_shapes=[
            pltpu.VMEM((segments.shape[0] // rows, rows), jnp.int32),
            pltpu.VMEM((heads, 2, rows, group * DH), bf16),
            pltpu.VMEM((heads, 2, rows, group * DH), bf16),
            pltpu.VMEM((heads, far + 2, rows, DH), bf16),
            pltpu.VMEM((heads, far + 2, rows, DH), bf16),
            pltpu.VMEM((2, span * rows, rows), f32),
            pltpu.VMEM((heads, 2, span * rows, HQ // KVH * rows), bf16),
            pltpu.VMEM((heads, 2, far + 2, rows, DH), f32),
            pltpu.VMEM((2, span * rows, group * rows), f32),
            pltpu.VMEM((far, heads, 2, rows, DH), bf16),
            pltpu.VMEM((2, heads, 2, rows, DH), bf16),
            pltpu.VMEM((reach, 2, heads, 2, rows, DH), bf16),
            pltpu.VMEM((heads, 2, 2, rows, DH), bf16),
            pltpu.VMEM((heads, 2, rows, DH), bf16),
            pltpu.VMEM((2, rows, qhalf), bf16),
            dma((heads + 1, 2)),
            dma((1,)),
            dma((heads, 2)),
            dma((2,)),
            dma((2, heads, 2)),
            dma((2, heads)),
            dma((2,)),
            dma((reach, heads, 2)),
            dma((2, heads, 2)),
            dma((heads,)),
            dma((heads,)),
            dma((3,)),
        ],
        compiler_params=pltpu.CompilerParams(
            collective_id=0, has_side_effects=True, vmem_limit_bytes=32 * 1024 * 1024
        ),
    )(*operands)
    return pl.pallas_call(
        emit,
        out_shape=shapes,
        in_specs=[pl.BlockSpec(memory_space=pl.ANY)] * 3,
        out_specs=[hbm] * 3,
        scratch_shapes=[dma((3,))],
        compiler_params=pltpu.CompilerParams(vmem_limit_bytes=1024 * 1024),
    )(*results)


def emit(a, b, c, a_out, b_out, c_out, sems):
    copies = [
        pltpu.make_async_copy(src, dst, sems.at[i])
        for i, (src, dst) in enumerate(((a, a_out), (b, b_out), (c, c_out)))
    ]
    for copy in copies:
        copy.start()
    for copy in copies:
        copy.wait()


def solution(mesh):
    split = P("section", "ctx", None)
    return jax.shard_map(
        local,
        mesh=mesh,
        in_specs=(split, split, split, split, P()),
        out_specs=(split, split, split),
        check_vma=False,
    )
```

```python
import functools
import math

import jax
import jax.numpy as jnp
from jax import lax
from jax.experimental import pallas as pl
from jax.experimental.pallas import tpu as pltpu
from jax.sharding import PartitionSpec as P

HQ = 8
KVH = 4
DH = 256
WINDOW = 512

MESH = pl.DeviceIdType.MESH
masked_score = -1e30


def kernel(
    count, reach, rows,
    q_in, k_in, v_in, g_in, seg_in,
    dq_out, dk_out, dv_out,
    seg_ref, kv_own, qb, gb, kb, vb, bias, dsb, acc, probs, sbuf, mbuf, rbuf, pbuf, rpart, dqb,
    local_sem, stage_sem, seg_sem, part_send, kv_send, kv_recv, pass_send,
    grad_send, grad_recv, mid_recv, gpart_send, gpart_recv, dq_sem,
):
    bf16, f32 = jnp.bfloat16, jnp.float32
    pairs = count // 2
    far = 2 * reach
    span = far + 1
    heads = KVH // 2
    qhalf = HQ // 2 * DH
    group = HQ // KVH
    me = lax.axis_index("ctx")
    c = me // 2
    k = me % 2
    other = 1 - k
    partner = 2 * c + other
    odd = c % 2 == 1
    even = c % 2 == 0
    beside = c + 1 - 2 * (c % 2)
    behind = c >= 2
    ahead = c + 2 < pairs
    hop = odd & (c + 1 < pairs)
    direct = [(0, 0, [(1, 1, 0), (1, 1, 1)], hop & (c % 4 == 1)), (1, 0, [(1, 1, 1)], hop & (c % 4 == 3))]

    def dev(index):
        return {"ctx": index}

    def cols(index, width):
        return pl.ds(pl.multiple_of(index * width, width), width)

    barrier = pltpu.get_barrier_semaphore()
    pl.semaphore_signal(barrier, inc=1, device_id=dev(partner), device_id_type=MESH)
    for j in range(2):
        pl.semaphore_signal(
            barrier, inc=1, device_id=dev(2 * beside + j), device_id_type=MESH
        )
    for there, ok in ((c - 2, behind), (c + 2, ahead)):

        @pl.when(ok)
        def _():
            for j in range(2):
                pl.semaphore_signal(
                    barrier, inc=1, device_id=dev(2 * there + j), device_id_type=MESH
                )

    @pl.when(even & (c >= 1) & (k == 1))
    def _():
        for j in range(2):
            pl.semaphore_signal(
                barrier, inc=1, device_id=dev(2 * (c - 1) + j), device_id_type=MESH
            )

    greeted = 3 + jnp.where(behind, 2, 0) + jnp.where(ahead, 2, 0) + jnp.where(hop, 1, 0)

    def blocks(number):
        return {
            1: sbuf.at[0, 0, 0], 2: sbuf.at[0, 0], 4: sbuf.at[0], 8: sbuf.at[pl.ds(0, 2)]
        }[number]

    def sent(sem, ref):
        pltpu.make_async_remote_copy(
            src_ref=ref, dst_ref=ref, send_sem=sem, recv_sem=sem,
            device_id=dev(partner), device_id_type=MESH,
        ).wait_send()

    def landed(sem, ref):
        pltpu.make_async_remote_copy(
            src_ref=ref, dst_ref=ref, send_sem=sem, recv_sem=sem,
            device_id=dev(partner), device_id_type=MESH,
        ).wait_recv()

    def kv_copy(which, d, j, g):
        return pltpu.make_async_remote_copy(
            src_ref=kv_own.at[which, j * heads + g],
            dst_ref=(kb, vb)[which].at[g, far - 2 * d + k],
            send_sem=kv_send.at[d - 1],
            recv_sem=kv_recv.at[which, g, d - 1],
            device_id=dev(2 * (c + d) + j),
            device_id_type=MESH,
        )

    def kv_landed(which, d, g):
        landed(kv_recv.at[which, g, d - 1], (kb, vb)[which].at[g, pl.ds(far - 2 * d, 2)])

    def pass_copy(which, g):
        ref = (kb, vb)[which]
        return pltpu.make_async_remote_copy(
            src_ref=ref.at[g, pl.ds(0, 2)],
            dst_ref=ref.at[g, pl.ds(far - 2, 2)],
            send_sem=pass_send.at[0],
            recv_sem=kv_recv.at[which, g, 0],
            device_id=dev(2 * beside + k),
            device_id_type=MESH,
        )

    for head in (0, 2, 1, 3):
        for which, src in enumerate((k_in, v_in)):
            pltpu.make_async_copy(
                src.at[0, :, pl.ds(head * DH, DH)], kv_own.at[which, head], stage_sem.at[0]
            ).start()
    seg_copy = pltpu.make_async_copy(seg_in, seg_ref, seg_sem.at[0])
    seg_copy.start()
    swaps = ((q_in, qb, group * DH, 0), (g_in, gb, group * DH, 0), (k_in, kb, DH, far), (v_in, vb, DH, far))
    own = [
        [
            pltpu.make_async_copy(
                src.at[0, :, cols(k * heads + g, width)], dst.at[g, base + k], local_sem.at[g, i // 3]
            )
            for i, (src, dst, width, base) in enumerate(swaps)
        ]
        for g in range(heads)
    ]
    for copy in own[0] + own[1]:
        copy.start()

    @pl.when(c < 2)
    def _():
        for slot in range(2):
            kb[:, slot] = jnp.zeros((heads, rows, DH), bf16)
            vb[:, slot] = jnp.zeros((heads, rows, DH), bf16)

    @pl.when(c == 0)
    def _():
        for slot in range(2, far):
            kb[:, slot] = jnp.zeros((heads, rows, DH), bf16)
            vb[:, slot] = jnp.zeros((heads, rows, DH), bf16)

    @pl.when(odd)
    def _():
        rbuf[0] = jnp.zeros(rbuf.shape[1:], bf16)

    @pl.when(c + 2 >= pairs)
    def _():
        rbuf[1] = jnp.zeros(rbuf.shape[1:], bf16)

    pltpu.make_async_copy(kv_own, kv_own, stage_sem.at[0]).wait()
    pl.semaphore_wait(barrier, greeted)

    swap = [
        [
            pltpu.make_async_remote_copy(
                src_ref=src.at[0, :, cols(other * heads + g, width)],
                dst_ref=dst.at[g, base + k],
                send_sem=part_send.at[0],
                recv_sem=local_sem.at[g, i // 3],
                device_id=dev(partner),
                device_id_type=MESH,
            )
            for i, (src, dst, width, base) in enumerate(swaps)
        ]
        for g in range(heads)
    ]
    for g in range(heads):
        for j in range(2):
            for which in range(2):
                for d, ok in ((2, ahead), (1, even)):

                    @pl.when(ok)
                    def _():
                        kv_copy(which, d, j, g).start()

            for *after, copies, ok in direct:
                if after == [g, j]:

                    @pl.when(ok)
                    def _():
                        for head, core, which in copies:
                            kv_copy(which, 1, core, head).start()

        for copy in swap[g]:
            copy.start()

    def seg_row(slot):
        block = jnp.maximum(2 * c - far + slot, 0)
        return seg_ref[pl.ds(block, 1), :].astype(f32)

    seg_copy.wait()
    key_local = lax.broadcasted_iota(jnp.int32, (rows, rows), 0)
    query_local = lax.broadcasted_iota(jnp.int32, (rows, rows), 1)
    for slot in range(far + 2):
        key_seg = jnp.broadcast_to(seg_row(slot), (rows, rows)).T
        exists = 2 * c - far + slot >= 0
        for qi in range(2):
            at = slot - qi
            if 0 <= at < span:
                back = (far - at) * rows + query_local - key_local
                same = key_seg == jnp.broadcast_to(seg_row(far + qi), (rows, rows))
                allowed = (back >= 0) & (back < WINDOW) & same & exists
                bias[qi, pl.ds(at * rows, rows), :] = jnp.where(allowed, 0.0, masked_score)

    def passed(which, g):
        if g == 0:
            return k >= 0
        skipped = (c % 4 == 3) | (which == 1)
        return (k == 0) | jnp.logical_not(skipped)

    def relay(g):
        @pl.when(odd & behind)
        def _():
            for which in range(2):
                kv_landed(which, 2, g)

                @pl.when(passed(which, g))
                def _():
                    pass_copy(which, g).start()

    def arrive(g, which):
        @pl.when(even & behind)
        def _():
            kv_landed(which, 2, g)

        exchanged = kb.at[0, pl.ds(0, 2)] if which else kb.at[:, pl.ds(0, 2 * group + 1)]
        landed(local_sem.at[g, which], exchanged)

        @pl.when(c >= 1)
        def _():
            kv_landed(which, 1, g)

    factor = DH**-0.5
    exponent = factor * math.log2(math.e)

    def stacked(ref, qi, g):
        return jnp.concatenate(
            [ref[g, qi, :, pl.ds(h * DH, DH)] for h in range(group)], axis=0
        )

    def keys(ref, qi, g):
        return ref[g, pl.ds(qi, span)].reshape(span * rows, DH)

    def nt(a, b):
        return lax.dot_general(a, b, (((1,), (1,)), ((), ())), preferred_element_type=f32)

    def slot_of(g, which):
        return 2 - which if g else 0

    def grad_copy(d, j, g, which, part=pl.ds(0, rows)):
        return pltpu.make_async_remote_copy(
            src_ref=sbuf.at[far - 2 * d + j, g, which, part],
            dst_ref=rbuf.at[d - 1, k, g, which, part],
            send_sem=grad_send.at[d - 1],
            recv_sem=grad_recv.at[d - 1, slot_of(g, which)],
            device_id=dev(2 * (c - d) + j),
            device_id_type=MESH,
        )

    def mid_copies(g, which):
        cuts = 2
        size = rows // cuts
        parts = [(pl.ds(j, 1), pl.ds(h * size, size)) for h in range(cuts) for j in range(2)]
        first = 8 * g + 4 * (1 - which)
        return [
            (
                js,
                part,
                pltpu.make_async_remote_copy(
                    src_ref=sbuf.at[pl.ds(far - 2 + js.start, js.size), g, which, part],
                    dst_ref=mbuf.at[js, g, which, part],
                    send_sem=grad_send.at[0],
                    recv_sem=mid_recv.at[first + i],
                    device_id=dev(2 * beside + k),
                    device_id_type=MESH,
                ),
            )
            for i, (js, part) in enumerate(parts)
        ]

    def part_copy(g):
        return pltpu.make_async_remote_copy(
            src_ref=pbuf.at[g, other],
            dst_ref=rpart.at[g],
            send_sem=gpart_send.at[0],
            recv_sem=gpart_recv.at[g],
            device_id=dev(partner),
            device_id_type=MESH,
        )

    def combine(g, which):
        @pl.when(odd & behind)
        def _():
            for js, part, copy in mid_copies(g, which):
                copy.wait_recv()
                for j in range(js.start, js.start + js.size):
                    total = acc[g, which, j, part] + mbuf[j, g, which, part].astype(f32)
                    sbuf[j, g, which, part] = total.astype(bf16)
                    grad_copy(2, j, g, which, part).start()

    def place(g, qi, which, part):
        for at in range(span):
            slot = at + qi
            piece = part[at * rows : (at + 1) * rows]
            if qi == 0 and slot > 0:
                acc[g, which, slot] = piece
                continue
            if qi == 1 and slot < far + 1:
                piece = acc[g, which, slot] + piece
            if slot < 2:
                acc[g, which, slot] = piece
            elif slot < far:
                sbuf[slot, g, which] = piece.astype(bf16)
            else:
                acc[g, which, slot] = piece
                pbuf[g, slot - far, which] = piece.astype(bf16)

    def send_even(g, which):
        @pl.when(even & behind)
        def _():
            for *_, copy in mid_copies(g, which):
                copy.start()
            for j in range(2):
                sbuf[j, g, which] = acc[g, which, j].astype(bf16)

    low = c % 4 == 0
    high = c % 4 == 2
    every = c >= 0
    far_plan = [(0, 1, 0, high), (0, 0, 1, high), (0, 1, 2, low), (0, 0, 2, low), (1, 1, 3, every), (1, 0, 4, every)]

    def send_far(point):
        for g, which, when, ok in far_plan:
            if when == point:

                @pl.when(even & behind & ok)
                def _():
                    for j in range(2):
                        grad_copy(2, j, g, which).start()

    for g in range(heads):
        if g == 0:
            relay(0)
        arrive(g, 0)
        if g == 1:
            combine(0, 1)
            send_far(2)
        for qi in range(2):
            q_rows, g_rows = stacked(qb, qi, g), stacked(gb, qi, g)
            mask = bias[qi]
            scores = nt(keys(kb, qi, g), q_rows) + jnp.concatenate([mask] * group, axis=1)
            top = jnp.max(scores, axis=0, keepdims=True)
            terms = jnp.exp2((scores - top) * exponent)
            inverse = 1.0 / jnp.sum(terms, axis=0, keepdims=True)
            prob = terms * inverse
            probs[qi] = prob
            dv = jnp.dot(prob.astype(bf16), g_rows, preferred_element_type=f32)
            place(g, qi, 1, dv)
        send_even(g, 1)
        send_far(3 * g)
        arrive(g, 1)
        for qi in range(2):
            q_rows, g_rows = stacked(qb, qi, g), stacked(gb, qi, g)
            prob = probs[qi]
            prob_grad = nt(keys(vb, qi, g), g_rows)
            delta = jnp.sum(prob * prob_grad, axis=0, keepdims=True)
            grad = (prob * (prob_grad - delta)).astype(bf16)
            dsb[g, qi] = grad
            dk = jnp.dot(grad, q_rows, preferred_element_type=f32) * factor
            place(g, qi, 0, dk)
        send_even(g, 0)
        send_far(3 * g + 1)

        if g == 0:
            relay(1)

        @pl.when(odd)
        def _():
            for which in (1, 0):
                for j in range(2):
                    grad_copy(1, j, g, which).start()

        part_copy(g).start()

    combine(0, 0)
    for qi in range(2):
        for g in range(heads):
            dq = lax.dot_general(
                dsb[g, qi], keys(kb, qi, g), (((0,), (0,)), ((), ())), preferred_element_type=f32
            )
            dq = (dq * factor).astype(bf16)
            for h in range(group):
                dqb[qi, :, pl.ds((group * g + h) * DH, DH)] = dq[h * rows : (h + 1) * rows]
    dq_local = pltpu.make_async_copy(dqb.at[k], dq_out.at[0, :, cols(k, qhalf)], dq_sem.at[0])
    dq_local.start()
    dq_remote = pltpu.make_async_remote_copy(
        src_ref=dqb.at[other],
        dst_ref=dq_out.at[0, :, cols(k, qhalf)],
        send_sem=dq_sem.at[1],
        recv_sem=dq_sem.at[0],
        device_id=dev(partner),
        device_id_type=MESH,
    )
    dq_remote.start()
    combine(1, 1)
    combine(1, 0)

    for g in range(heads):
        part_copy(g).wait_recv()
        for which, out in ((1, dv_out), (0, dk_out)):
            for d, ok in ((1, even), (2, ahead)):
                if g or which:

                    @pl.when(ok)
                    def _():
                        ref = rbuf.at[d - 1, :, g, which] if g else rbuf.at[d - 1, :, g]
                        landed(grad_recv.at[d - 1, slot_of(g, which)], ref)

            mine = acc[g, which, far + k]
            theirs = rpart[g, which].astype(f32)
            for d in range(reach):
                mine += rbuf[d, k, g, which].astype(f32)
                theirs += rbuf[d, other, g, which].astype(f32)
            out[0, :, cols(k * heads + g, DH)] = mine.astype(bf16)
            out[0, :, cols(other * heads + g, DH)] = theirs.astype(bf16)

    sent(part_send.at[0], kb)
    sent(gpart_send.at[0], blocks(4))
    for d, ok in ((2, ahead), (1, even)):

        @pl.when(ok)
        def _():
            sent(kv_send.at[d - 1], blocks(8))

    for *_, copies, ok in direct:

        @pl.when(ok)
        def _():
            sent(kv_send.at[0], blocks(len(copies)))

    upper = odd & behind & (k == 1)
    for number, ok in (
        (8, odd & behind & (k == 0)), (6, upper & (c % 4 == 1)), (4, upper & (c % 4 == 3))
    ):

        @pl.when(ok)
        def _():
            sent(pass_send.at[0], kb.at[0] if number == 6 else blocks(number))

    for d, ok in ((2, behind), (1, odd | behind)):

        @pl.when(ok)
        def _():
            sent(grad_send.at[d - 1], blocks(8))

    landed(dq_sem.at[0], dqb)
    dq_remote.wait_send()


def local(queries, key_states, value_states, upstream, segments):
    count = lax.axis_size("ctx")
    sections = lax.axis_size("section")
    rows = queries.shape[1]
    out_grad = upstream
    if sections > 1:
        out_grad = lax.ppermute(
            upstream, "section", [(i, (i - 1) % sections) for i in range(sections)]
        )
    reach = -(-(WINDOW - 1) // (2 * rows))
    assert reach == 2 and count % 4 == 0
    far = 2 * reach
    span = far + 1
    heads = KVH // 2
    group = HQ // KVH
    qhalf = HQ // 2 * DH
    bf16, f32 = jnp.bfloat16, jnp.float32
    dma = pltpu.SemaphoreType.DMA
    hbm = pl.BlockSpec(memory_space=pltpu.HBM)
    vmem = pl.BlockSpec(memory_space=pltpu.VMEM)
    shapes = (
        jax.ShapeDtypeStruct(queries.shape, bf16),
        jax.ShapeDtypeStruct(key_states.shape, bf16),
        jax.ShapeDtypeStruct(value_states.shape, bf16),
    )
    operands = (queries, key_states, value_states, out_grad, segments.reshape(-1, rows))
    operands = [pltpu.with_memory_space_constraint(x, pltpu.HBM) for x in operands]
    results = pl.pallas_call(
        functools.partial(kernel, count, reach, rows),
        out_shape=shapes,
        in_specs=[hbm] * 5,
        out_specs=(vmem, vmem, vmem),
        scratch_shapes=[
            pltpu.VMEM((segments.shape[0] // rows, rows), jnp.int32),
            pltpu.VMEM((2, KVH, rows, DH), bf16),
            pltpu.VMEM((heads, 2, rows, group * DH), bf16),
            pltpu.VMEM((heads, 2, rows, group * DH), bf16),
            pltpu.VMEM((heads, far + 2, rows, DH), bf16),
            pltpu.VMEM((heads, far + 2, rows, DH), bf16),
            pltpu.VMEM((2, span * rows, rows), f32),
            pltpu.VMEM((heads, 2, span * rows, HQ // KVH * rows), bf16),
            pltpu.VMEM((heads, 2, far + 2, rows, DH), f32),
            pltpu.VMEM((2, span * rows, group * rows), f32),
            pltpu.VMEM((far, heads, 2, rows, DH), bf16),
            pltpu.VMEM((2, heads, 2, rows, DH), bf16),
            pltpu.VMEM((reach, 2, heads, 2, rows, DH), bf16),
            pltpu.VMEM((heads, 2, 2, rows, DH), bf16),
            pltpu.VMEM((heads, 2, rows, DH), bf16),
            pltpu.VMEM((2, rows, qhalf), bf16),
            dma((heads, 2)),
            dma((1,)),
            dma((1,)),
            dma((1,)),
            dma((2,)),
            dma((2, heads, 2)),
            dma((1,)),
            dma((2,)),
            dma((reach, 3)),
            dma((16,)),
            dma((1,)),
            dma((heads,)),
            dma((2,)),
        ],
        compiler_params=pltpu.CompilerParams(
            collective_id=0, has_side_effects=True, vmem_limit_bytes=32 * 1024 * 1024
        ),
    )(*operands)
    return pl.pallas_call(
        emit,
        out_shape=shapes,
        in_specs=[pl.BlockSpec(memory_space=pl.ANY)] * 3,
        out_specs=[hbm] * 3,
        scratch_shapes=[dma((3,))],
        compiler_params=pltpu.CompilerParams(vmem_limit_bytes=1024 * 1024),
    )(*results)


def emit(a, b, c, a_out, b_out, c_out, sems):
    copies = [
        pltpu.make_async_copy(src, dst, sems.at[i])
        for i, (src, dst) in enumerate(((a, a_out), (b, b_out), (c, c_out)))
    ]
    for copy in copies:
        copy.start()
    for copy in copies:
        copy.wait()


def solution(mesh):
    split = P("section", "ctx", None)
    return jax.shard_map(
        local,
        mesh=mesh,
        in_specs=(split, split, split, split, P()),
        out_specs=(split, split, split),
        check_vma=False,
    )
```

```python
import functools
import math

import jax
import jax.numpy as jnp
from jax import lax
from jax.experimental import pallas as pl
from jax.experimental.pallas import tpu as pltpu
from jax.sharding import PartitionSpec as P

HQ = 8
KVH = 4
DH = 256
WINDOW = 512

MESH = pl.DeviceIdType.MESH
masked_score = -1e30


def kernel(
    count, reach, rows,
    q_in, k_in, v_in, g_in, seg_in,
    dq_out, dk_out, dv_out,
    seg_ref, kv_own, qb, gb, kb, vb, bias, dsb, acc, probs, sbuf, mbuf, rbuf, pbuf, rpart, dqb,
    local_sem, stage_sem, seg_sem, part_send, kv_send, kv_recv, pass_send,
    grad_send, grad_recv, mid_recv, gpart_send, gpart_recv, dq_sem,
):
    bf16, f32 = jnp.bfloat16, jnp.float32
    pairs = count // 2
    far = 2 * reach
    span = far + 1
    heads = KVH // 2
    qhalf = HQ // 2 * DH
    group = HQ // KVH
    me = lax.axis_index("ctx")
    c = me // 2
    k = me % 2
    other = 1 - k
    partner = 2 * c + other
    odd = c % 2 == 1
    even = c % 2 == 0
    beside = c + 1 - 2 * (c % 2)
    behind = c >= 2
    ahead = c + 2 < pairs
    hop = odd & (c + 1 < pairs)
    direct = [(0, 0, [(1, 1, 0), (1, 1, 1)], hop & (c % 4 == 1)), (1, 0, [(1, 1, 1)], hop & (c % 4 == 3))]

    def dev(index):
        return {"ctx": index}

    def cols(index, width):
        return pl.ds(pl.multiple_of(index * width, width), width)

    barrier = pltpu.get_barrier_semaphore()
    pl.semaphore_signal(barrier, inc=1, device_id=dev(partner), device_id_type=MESH)
    for j in range(2):
        pl.semaphore_signal(
            barrier, inc=1, device_id=dev(2 * beside + j), device_id_type=MESH
        )
    for there, ok in ((c - 2, behind), (c + 2, ahead)):

        @pl.when(ok)
        def _():
            for j in range(2):
                pl.semaphore_signal(
                    barrier, inc=1, device_id=dev(2 * there + j), device_id_type=MESH
                )

    @pl.when(even & (c >= 1) & (k == 1))
    def _():
        for j in range(2):
            pl.semaphore_signal(
                barrier, inc=1, device_id=dev(2 * (c - 1) + j), device_id_type=MESH
            )

    greeted = 3 + jnp.where(behind, 2, 0) + jnp.where(ahead, 2, 0) + jnp.where(hop, 1, 0)

    def blocks(number):
        return {
            1: sbuf.at[0, 0, 0], 2: sbuf.at[0, 0], 4: sbuf.at[0], 8: sbuf.at[pl.ds(0, 2)]
        }[number]

    def sent(sem, ref):
        pltpu.make_async_remote_copy(
            src_ref=ref, dst_ref=ref, send_sem=sem, recv_sem=sem,
            device_id=dev(partner), device_id_type=MESH,
        ).wait_send()

    def landed(sem, ref):
        pltpu.make_async_remote_copy(
            src_ref=ref, dst_ref=ref, send_sem=sem, recv_sem=sem,
            device_id=dev(partner), device_id_type=MESH,
        ).wait_recv()

    def kv_copy(which, d, j, g):
        return pltpu.make_async_remote_copy(
            src_ref=kv_own.at[which, j * heads + g],
            dst_ref=(kb, vb)[which].at[g, far - 2 * d + k],
            send_sem=kv_send.at[d - 1],
            recv_sem=kv_recv.at[which, g, d - 1],
            device_id=dev(2 * (c + d) + j),
            device_id_type=MESH,
        )

    def kv_landed(which, d, g):
        landed(kv_recv.at[which, g, d - 1], (kb, vb)[which].at[g, pl.ds(far - 2 * d, 2)])

    def pass_copy(which, g):
        ref = (kb, vb)[which]
        return pltpu.make_async_remote_copy(
            src_ref=ref.at[g, pl.ds(0, 2)],
            dst_ref=ref.at[g, pl.ds(far - 2, 2)],
            send_sem=pass_send.at[0],
            recv_sem=kv_recv.at[which, g, 0],
            device_id=dev(2 * beside + k),
            device_id_type=MESH,
        )

    for head in (0, 2, 1, 3):
        for which, src in enumerate((k_in, v_in)):
            pltpu.make_async_copy(
                src.at[0, :, pl.ds(head * DH, DH)], kv_own.at[which, head], stage_sem.at[0]
            ).start()
    seg_copy = pltpu.make_async_copy(seg_in, seg_ref, seg_sem.at[0])
    seg_copy.start()
    swaps = ((q_in, qb, group * DH, 0), (g_in, gb, group * DH, 0), (k_in, kb, DH, far), (v_in, vb, DH, far))
    own = [
        [
            pltpu.make_async_copy(
                src.at[0, :, cols(k * heads + g, width)], dst.at[g, base + k], local_sem.at[g, i // 3]
            )
            for i, (src, dst, width, base) in enumerate(swaps)
        ]
        for g in range(heads)
    ]
    for copy in own[0] + own[1]:
        copy.start()

    @pl.when(c < 2)
    def _():
        for slot in range(2):
            kb[:, slot] = jnp.zeros((heads, rows, DH), bf16)
            vb[:, slot] = jnp.zeros((heads, rows, DH), bf16)

    @pl.when(c == 0)
    def _():
        for slot in range(2, far):
            kb[:, slot] = jnp.zeros((heads, rows, DH), bf16)
            vb[:, slot] = jnp.zeros((heads, rows, DH), bf16)

    @pl.when(odd)
    def _():
        rbuf[0] = jnp.zeros(rbuf.shape[1:], bf16)

    @pl.when(c + 2 >= pairs)
    def _():
        rbuf[1] = jnp.zeros(rbuf.shape[1:], bf16)

    def seg_row(slot):
        block = jnp.maximum(2 * c - far + slot, 0)
        return seg_ref[pl.ds(block, 1), :].astype(f32)

    seg_copy.wait()
    key_local = lax.broadcasted_iota(jnp.int32, (rows, rows), 0)
    query_local = lax.broadcasted_iota(jnp.int32, (rows, rows), 1)
    for slot in range(far + 2):
        key_seg = jnp.broadcast_to(seg_row(slot), (rows, rows)).T
        exists = 2 * c - far + slot >= 0
        for qi in range(2):
            at = slot - qi
            if 0 <= at < span:
                back = (far - at) * rows + query_local - key_local
                same = key_seg == jnp.broadcast_to(seg_row(far + qi), (rows, rows))
                allowed = (back >= 0) & (back < WINDOW) & same & exists
                bias[qi, pl.ds(at * rows, rows), :] = jnp.where(allowed, 0.0, masked_score)

    pltpu.make_async_copy(kv_own, kv_own, stage_sem.at[0]).wait()
    pl.semaphore_wait(barrier, greeted)

    swap = [
        [
            pltpu.make_async_remote_copy(
                src_ref=src.at[0, :, cols(other * heads + g, width)],
                dst_ref=dst.at[g, base + k],
                send_sem=part_send.at[0],
                recv_sem=local_sem.at[g, i // 3],
                device_id=dev(partner),
                device_id_type=MESH,
            )
            for i, (src, dst, width, base) in enumerate(swaps)
        ]
        for g in range(heads)
    ]
    for g in range(heads):
        for j in range(2):
            for which in range(2):
                for d, ok in ((2, ahead), (1, even)):

                    @pl.when(ok)
                    def _():
                        kv_copy(which, d, j, g).start()

            for *after, copies, ok in direct:
                if after == [g, j]:

                    @pl.when(ok)
                    def _():
                        for head, core, which in copies:
                            kv_copy(which, 1, core, head).start()

        for copy in swap[g]:
            copy.start()

    def passed(which, g):
        if g == 0:
            return k >= 0
        skipped = (c % 4 == 3) | (which == 1)
        return (k == 0) | jnp.logical_not(skipped)

    def relay(g):
        @pl.when(odd & behind)
        def _():
            for which in range(2):
                kv_landed(which, 2, g)

                @pl.when(passed(which, g))
                def _():
                    pass_copy(which, g).start()

    def arrive(g, which):
        @pl.when(even & behind)
        def _():
            kv_landed(which, 2, g)

        exchanged = kb.at[0, pl.ds(0, 2)] if which else kb.at[:, pl.ds(0, 2 * group + 1)]
        landed(local_sem.at[g, which], exchanged)

        @pl.when(c >= 1)
        def _():
            kv_landed(which, 1, g)

    factor = DH**-0.5
    exponent = factor * math.log2(math.e)

    def stacked(ref, qi, g):
        return jnp.concatenate(
            [ref[g, qi, :, pl.ds(h * DH, DH)] for h in range(group)], axis=0
        )

    def keys(ref, qi, g):
        return ref[g, pl.ds(qi, span)].reshape(span * rows, DH)

    def nt(a, b):
        return lax.dot_general(a, b, (((1,), (1,)), ((), ())), preferred_element_type=f32)

    def slot_of(g, which):
        return 2 - which if g else 0

    def grad_copy(d, j, g, which, part=pl.ds(0, rows)):
        return pltpu.make_async_remote_copy(
            src_ref=sbuf.at[far - 2 * d + j, g, which, part],
            dst_ref=rbuf.at[d - 1, k, g, which, part],
            send_sem=grad_send.at[d - 1],
            recv_sem=grad_recv.at[d - 1, slot_of(g, which)],
            device_id=dev(2 * (c - d) + j),
            device_id_type=MESH,
        )

    def mid_copies(g, which):
        cuts = 2
        size = rows // cuts
        parts = [(pl.ds(j, 1), pl.ds(h * size, size)) for h in range(cuts) for j in range(2)]
        first = 8 * g + 4 * (1 - which)
        return [
            (
                js,
                part,
                pltpu.make_async_remote_copy(
                    src_ref=sbuf.at[pl.ds(far - 2 + js.start, js.size), g, which, part],
                    dst_ref=mbuf.at[js, g, which, part],
                    send_sem=grad_send.at[0],
                    recv_sem=mid_recv.at[first + i],
                    device_id=dev(2 * beside + k),
                    device_id_type=MESH,
                ),
            )
            for i, (js, part) in enumerate(parts)
        ]

    def part_copy(g):
        return pltpu.make_async_remote_copy(
            src_ref=pbuf.at[g, other],
            dst_ref=rpart.at[g],
            send_sem=gpart_send.at[0],
            recv_sem=gpart_recv.at[g],
            device_id=dev(partner),
            device_id_type=MESH,
        )

    def combine(g, which):
        @pl.when(odd & behind)
        def _():
            for js, part, copy in mid_copies(g, which):
                copy.wait_recv()
                for j in range(js.start, js.start + js.size):
                    total = acc[g, which, j, part] + mbuf[j, g, which, part].astype(f32)
                    sbuf[j, g, which, part] = total.astype(bf16)
                    grad_copy(2, j, g, which, part).start()

    def place(g, qi, which, part):
        for at in range(span):
            slot = at + qi
            piece = part[at * rows : (at + 1) * rows]
            if qi == 0 and slot > 0:
                acc[g, which, slot] = piece
                continue
            if qi == 1 and slot < far + 1:
                piece = acc[g, which, slot] + piece
            if slot < 2:
                acc[g, which, slot] = piece
            elif slot < far:
                sbuf[slot, g, which] = piece.astype(bf16)
            else:
                acc[g, which, slot] = piece
                pbuf[g, slot - far, which] = piece.astype(bf16)

    def send_even(g, which):
        @pl.when(even & behind)
        def _():
            for *_, copy in mid_copies(g, which):
                copy.start()
            for j in range(2):
                sbuf[j, g, which] = acc[g, which, j].astype(bf16)

    low = c % 4 == 0
    high = c % 4 == 2
    every = c >= 0
    far_plan = [(0, 1, 0, high), (0, 0, 1, high), (0, 1, 2, low), (0, 0, 2, low), (1, 1, 3, every), (1, 0, 4, every)]

    def send_far(point):
        for g, which, when, ok in far_plan:
            if when == point:

                @pl.when(even & behind & ok)
                def _():
                    for j in range(2):
                        grad_copy(2, j, g, which).start()

    for g in range(heads):
        if g == 0:
            relay(0)
        arrive(g, 0)
        if g == 1:
            combine(0, 1)
            send_far(2)
        for qi in range(2):
            q_rows, g_rows = stacked(qb, qi, g), stacked(gb, qi, g)
            mask = bias[qi]
            scores = nt(keys(kb, qi, g), q_rows) + jnp.concatenate([mask] * group, axis=1)
            top = jnp.max(scores, axis=0, keepdims=True)
            terms = jnp.exp2((scores - top) * exponent)
            inverse = 1.0 / jnp.sum(terms, axis=0, keepdims=True)
            prob = terms * inverse
            probs[qi] = prob
            dv = jnp.dot(prob.astype(bf16), g_rows, preferred_element_type=f32)
            place(g, qi, 1, dv)
        send_even(g, 1)
        send_far(3 * g)
        arrive(g, 1)
        for qi in range(2):
            q_rows, g_rows = stacked(qb, qi, g), stacked(gb, qi, g)
            prob = probs[qi]
            prob_grad = nt(keys(vb, qi, g), g_rows)
            delta = jnp.sum(prob * prob_grad, axis=0, keepdims=True)
            grad = (prob * (prob_grad - delta)).astype(bf16)
            dsb[g, qi] = grad
            dk = jnp.dot(grad, q_rows, preferred_element_type=f32) * factor
            place(g, qi, 0, dk)
        send_even(g, 0)
        send_far(3 * g + 1)

        if g == 0:
            relay(1)

        @pl.when(odd)
        def _():
            for which in (1, 0):
                for j in range(2):
                    grad_copy(1, j, g, which).start()

        part_copy(g).start()

    combine(0, 0)
    for qi in range(2):
        for g in range(heads):
            dq = lax.dot_general(
                dsb[g, qi], keys(kb, qi, g), (((0,), (0,)), ((), ())), preferred_element_type=f32
            )
            dq = (dq * factor).astype(bf16)
            for h in range(group):
                dqb[qi, :, pl.ds((group * g + h) * DH, DH)] = dq[h * rows : (h + 1) * rows]
    dq_local = pltpu.make_async_copy(dqb.at[k], dq_out.at[0, :, cols(k, qhalf)], dq_sem.at[0])
    dq_local.start()
    dq_remote = pltpu.make_async_remote_copy(
        src_ref=dqb.at[other],
        dst_ref=dq_out.at[0, :, cols(k, qhalf)],
        send_sem=dq_sem.at[1],
        recv_sem=dq_sem.at[0],
        device_id=dev(partner),
        device_id_type=MESH,
    )
    dq_remote.start()
    combine(1, 1)
    combine(1, 0)

    for g in range(heads):
        part_copy(g).wait_recv()
        for which, out in ((1, dv_out), (0, dk_out)):
            for d, ok in ((1, even), (2, ahead)):
                if g or which:

                    @pl.when(ok)
                    def _():
                        ref = rbuf.at[d - 1, :, g, which] if g else rbuf.at[d - 1, :, g]
                        landed(grad_recv.at[d - 1, slot_of(g, which)], ref)

            mine = acc[g, which, far + k]
            theirs = rpart[g, which].astype(f32)
            for d in range(reach):
                mine += rbuf[d, k, g, which].astype(f32)
                theirs += rbuf[d, other, g, which].astype(f32)
            out[0, :, cols(k * heads + g, DH)] = mine.astype(bf16)
            out[0, :, cols(other * heads + g, DH)] = theirs.astype(bf16)

    sent(part_send.at[0], kb)
    sent(gpart_send.at[0], blocks(4))
    for d, ok in ((2, ahead), (1, even)):

        @pl.when(ok)
        def _():
            sent(kv_send.at[d - 1], blocks(8))

    for *_, copies, ok in direct:

        @pl.when(ok)
        def _():
            sent(kv_send.at[0], blocks(len(copies)))

    upper = odd & behind & (k == 1)
    for number, ok in (
        (8, odd & behind & (k == 0)), (6, upper & (c % 4 == 1)), (4, upper & (c % 4 == 3))
    ):

        @pl.when(ok)
        def _():
            sent(pass_send.at[0], kb.at[0] if number == 6 else blocks(number))

    for d, ok in ((2, behind), (1, odd | behind)):

        @pl.when(ok)
        def _():
            sent(grad_send.at[d - 1], blocks(8))

    landed(dq_sem.at[0], dqb)
    dq_remote.wait_send()


def local(queries, key_states, value_states, upstream, segments):
    count = lax.axis_size("ctx")
    sections = lax.axis_size("section")
    rows = queries.shape[1]
    out_grad = upstream
    if sections > 1:
        out_grad = lax.ppermute(
            upstream, "section", [(i, (i - 1) % sections) for i in range(sections)]
        )
    reach = -(-(WINDOW - 1) // (2 * rows))
    assert reach == 2 and count % 4 == 0
    far = 2 * reach
    span = far + 1
    heads = KVH // 2
    group = HQ // KVH
    qhalf = HQ // 2 * DH
    bf16, f32 = jnp.bfloat16, jnp.float32
    dma = pltpu.SemaphoreType.DMA
    hbm = pl.BlockSpec(memory_space=pltpu.HBM)
    vmem = pl.BlockSpec(memory_space=pltpu.VMEM)
    shapes = (
        jax.ShapeDtypeStruct(queries.shape, bf16),
        jax.ShapeDtypeStruct(key_states.shape, bf16),
        jax.ShapeDtypeStruct(value_states.shape, bf16),
    )
    operands = (queries, key_states, value_states, out_grad, segments.reshape(-1, rows))
    operands = [pltpu.with_memory_space_constraint(x, pltpu.HBM) for x in operands]
    results = pl.pallas_call(
        functools.partial(kernel, count, reach, rows),
        out_shape=shapes,
        in_specs=[hbm] * 5,
        out_specs=(vmem, vmem, vmem),
        scratch_shapes=[
            pltpu.VMEM((segments.shape[0] // rows, rows), jnp.int32),
            pltpu.VMEM((2, KVH, rows, DH), bf16),
            pltpu.VMEM((heads, 2, rows, group * DH), bf16),
            pltpu.VMEM((heads, 2, rows, group * DH), bf16),
            pltpu.VMEM((heads, far + 2, rows, DH), bf16),
            pltpu.VMEM((heads, far + 2, rows, DH), bf16),
            pltpu.VMEM((2, span * rows, rows), f32),
            pltpu.VMEM((heads, 2, span * rows, HQ // KVH * rows), bf16),
            pltpu.VMEM((heads, 2, far + 2, rows, DH), f32),
            pltpu.VMEM((2, span * rows, group * rows), f32),
            pltpu.VMEM((far, heads, 2, rows, DH), bf16),
            pltpu.VMEM((2, heads, 2, rows, DH), bf16),
            pltpu.VMEM((reach, 2, heads, 2, rows, DH), bf16),
            pltpu.VMEM((heads, 2, 2, rows, DH), bf16),
            pltpu.VMEM((heads, 2, rows, DH), bf16),
            pltpu.VMEM((2, rows, qhalf), bf16),
            dma((heads, 2)),
            dma((1,)),
            dma((1,)),
            dma((1,)),
            dma((2,)),
            dma((2, heads, 2)),
            dma((1,)),
            dma((2,)),
            dma((reach, 3)),
            dma((16,)),
            dma((1,)),
            dma((heads,)),
            dma((2,)),
        ],
        compiler_params=pltpu.CompilerParams(
            collective_id=0, has_side_effects=True, vmem_limit_bytes=32 * 1024 * 1024
        ),
    )(*operands)
    return pl.pallas_call(
        emit,
        out_shape=shapes,
        in_specs=[pl.BlockSpec(memory_space=pl.ANY)] * 3,
        out_specs=[hbm] * 3,
        scratch_shapes=[dma((3,))],
        compiler_params=pltpu.CompilerParams(vmem_limit_bytes=1024 * 1024),
    )(*results)


def emit(a, b, c, a_out, b_out, c_out, sems):
    copies = [
        pltpu.make_async_copy(src, dst, sems.at[i])
        for i, (src, dst) in enumerate(((a, a_out), (b, b_out), (c, c_out)))
    ]
    for copy in copies:
        copy.start()
    for copy in copies:
        copy.wait()


def solution(mesh):
    split = P("section", "ctx", None)
    return jax.shard_map(
        local,
        mesh=mesh,
        in_specs=(split, split, split, split, P()),
        out_specs=(split, split, split),
        check_vma=False,
    )
```
